32 devices in a mesh: dp: 4 (over y, x), expert: 8 (over z, core).
Axes of the slice: x: 2, y: 2, z: 4, core: 2. Of those that a mesh axis runs over, the one named last changes fastest.
Arguments:
- tokens: bfloat16 [32, 256, 1280], P(('dp', 'expert')), may hold values from -6 to 6
- lengths: int32 [32], P(('dp', 'expert')), may hold values from 64 to 256, as said below
- routes: int32 [32, 256, 7], P(('dp', 'expert')), may hold values from 0 to 14, all different within a row; in each aligned block of 256 rows (0 to 255, 256 to 511, ..., all dimensions but the last counted through in order) at most 168 rows name the same one
- attn_gain: bfloat16 [1280], P('expert'), may hold values from 0.099609375 to 1.8984375
- query_weight: bfloat16 [1280, 1280], P('expert'), may hold values from -0.15625 to 0.15625
- key_weight: bfloat16 [1280, 1280], P('expert'), may hold values from -0.15625 to 0.15625
- value_weight: bfloat16 [1280, 1280], P('expert'), may hold values from -0.15625 to 0.15625
- out_weight: bfloat16 [1280, 1280], P('expert'), may hold values from -1.25 to 1.25
- ffn_gain: bfloat16 [1280], P('expert'), may hold values from 0.099609375 to 1.8984375
- shared_gate: bfloat16 [1280, 896], P('expert'), may hold values from -0.15625 to 0.15625
- shared_up: bfloat16 [1280, 896], P('expert'), may hold values from -0.15625 to 0.15625
- shared_down: bfloat16 [896, 1280], P('expert'), may hold values from -0.1875 to 0.1875
- router_weight: bfloat16 [1280, 15], P('expert'), may hold values from -0.15625 to 0.15625
- expert_gate: bfloat16 [16, 1280, 896], P('expert'), may hold values from -0.15625 to 0.15625
- expert_up: bfloat16 [16, 1280, 896], P('expert'), may hold values from -0.15625 to 0.15625
- expert_down: bfloat16 [16, 896, 1280], P('expert'), may hold values from -3.5 to 3.5
- cotangent: bfloat16 [32, 256, 1280], P(('dp', 'expert')), may hold values from -6 to 6
Outputs:
- output: bfloat16 [32, 256, 1280], P(('dp', 'expert'))
- grad_tokens: float32 [32, 256, 1280], P(('dp', 'expert'))
- grad_attn_gain: float32 [1280], P('expert')
- grad_query: float32 [1280, 1280], P('expert')
- grad_key: float32 [1280, 1280], P('expert')
- grad_value: float32 [1280, 1280], P('expert')
- grad_out: float32 [1280, 1280], P('expert')
- grad_ffn_gain: float32 [1280], P('expert')
- grad_shared_gate: float32 [1280, 896], P('expert')
- grad_shared_up: float32 [1280, 896], P('expert')
- grad_shared_down: float32 [896, 1280], P('expert')
- grad_router: float32 [1280, 15], P('expert')
- grad_expert_gate: float32 [16, 1280, 896], P('expert', 'dp')
- grad_expert_up: float32 [16, 1280, 896], P('expert', 'dp')
- grad_expert_down: float32 [16, 896, 1280], P('expert', 'dp')
The draws below stay inside these ranges and needn't reach their ends.
Inputs may be any that keep to these rules, and one draw needn't show every extreme that they name: `routes`: in each sequence, no expert is chosen by more than 168 of its token choices, and in some sequence one expert is chosen by exactly 168; every routed expert is chosen somewhere. `lengths`: some sequence has length exactly 256.
All inputs are finite; a program needn't handle non-finite values.
Results may differ from the reference program's by a relative error of at most 0.025.
Values may be sent and summed in bfloat16 or wider, within the bound.
No kernel may reach another device: no remote copies, remote signals or barrier semaphores. Data moves between devices by JAX's collectives and lax.ppermute only.
A program may use at most 320 MiB of HBM per device.

```python
import math
import jax
import jax.numpy as jnp
import numpy as np
from jax import lax

D = 1280
HEADS = 10
HEAD_DIM = 128
FF = 896
TOP = 7
SEQ = 256
SLOTS = 16
ROUTED = 15
SEQS = 32
CAP = 168


def draw_lengths(key, part):
    first_key, second_key = jax.random.split(jax.random.fold_in(key, 11))
    drawn = jax.random.randint(first_key, (SEQS,), SEQ // 4, SEQ + 1)
    longest = jax.random.randint(second_key, (), 0, SEQS)
    return jnp.where(jnp.arange(SEQS) == longest, SEQ, drawn).astype(jnp.int32)


def block_scale(own_key, extent, cuts, low, top_value):
    loudness, own = 1.0, jax.random.fold_in(own_key, 6)
    for axis_at, shards_of in cuts:
        steps = jnp.exp(jax.random.uniform(jax.random.fold_in(own, axis_at), (shards_of,), jnp.float32, low / len(cuts), top_value / len(cuts)))
        loudness = loudness * jnp.repeat(steps, extent[axis_at] // shards_of).reshape([-1 if axis == axis_at else 1 for axis in range(len(extent))])
    return loudness


def assign_block(rng, own, number, rows, amount, top, bound, skew):
    sequence = jax.random.permutation(rng, amount)
    crowded, common = shares(amount, rows * top, bound, skew, True), shares(amount, rows * top, bound, skew, False)
    places = jnp.arange(amount)

    def named(sizes, rotation):
        used = int((sizes > 0).sum())
        fixed = max(1, used // 4)
        passed = fixed + (places - fixed + rotation * (used - fixed)) % max(1, amount - fixed)
        return jnp.zeros((amount,), jnp.int32).at[sequence[jnp.where(places < fixed, places, passed)]].set(jnp.asarray(sizes, jnp.int32))

    sizes = jnp.where(number % 4 == 0, named(crowded, number // 4), named(common, number - number // 4 - 1))
    mixed = jax.random.permutation(jax.random.fold_in(own, 3), amount)
    donor, receiver = mixed[0:amount // 2 * 2:2], mixed[1:amount // 2 * 2:2]
    margin = jnp.minimum(sizes[donor] - 1, bound - sizes[receiver]) // 2
    margin = jnp.where((donor == sequence[0]) | (receiver == sequence[0]) | (sizes[receiver] == 0), 0, jnp.maximum(margin, 0))
    passed = jax.random.randint(jax.random.fold_in(own, 4), (amount // 2,), 0, 1 << 20) % (margin + 1)
    sizes = sizes.at[donor].add(-passed).at[receiver].add(passed)
    labels = jnp.searchsorted(jnp.cumsum(sizes), jnp.arange(rows * top), side="right").astype(jnp.int32)
    listing = labels.reshape(top, rows).T
    listing = listing[jax.random.permutation(jax.random.fold_in(own, 1), rows)]
    rotation = jax.random.randint(jax.random.fold_in(own, 2), (rows, 1), 0, top)
    return jnp.take_along_axis(listing, (jnp.arange(top)[None, :] + rotation) % top, axis=1)


def shares(amount, total, bound, lean, full):
    loads = [(1 << 20) // math.isqrt(rank ** lean) + 1 for rank in range(1, amount + 1)]
    largest = bound if full else min(bound, max(-(-total // amount), total * loads[0] // sum(loads)))
    least = 1 if total - largest >= amount - 1 else 0
    holding, surplus = [largest] + [least] * (amount - 1), total - largest - least * (amount - 1)
    while surplus > 0:
        candidates = [i for i in range(1, amount) if holding[i] < largest] or [i for i in range(1, amount) if holding[i] < bound]
        pool, left = sum([loads[i] for i in candidates]), surplus
        for i in candidates:
            extra = min(bound - holding[i], max(1, left * loads[i] // pool), surplus)
            holding[i] = holding[i] + extra
            surplus = surplus - extra
    return np.array(holding)


def noise(stream_key, dims, scale, bound, shards=(), kind=jnp.bfloat16):
    values = jax.random.normal(stream_key, dims, jnp.float32) * scale
    if len(shards) > 0:
        values = block_scale(stream_key, dims, shards, -0.22, 0.18) * values
    return jnp.clip(values, min=-bound, max=bound).astype(kind)


def setup_inputs(seed: int = 0) -> dict:
    keys = jax.random.split(jax.random.key(seed), 18)
    tokens = noise(keys[0], (SEQS, SEQ, D), 1.0, 6.0, ((0, 32),))
    lengths = draw_lengths(jax.random.fold_in(keys[17], 71), 0)
    routes_keys = jax.random.split(jax.random.fold_in(keys[2], 1), SEQS * SEQ // SEQ)
    routes_turns = jax.random.permutation(jax.random.fold_in(keys[2], 3), SEQS * SEQ // SEQ)
    routes = jax.vmap(lambda own, number: assign_block(jax.random.fold_in(keys[2], 2), own, number, SEQ, ROUTED, TOP, CAP, 1))(routes_keys, routes_turns).reshape((SEQS, SEQ, TOP))
    attn_gain = jnp.clip(1.0 + 0.18 * jax.random.normal(keys[3], (D,), jnp.float32), 0.099609375, 1.8984375).astype(jnp.bfloat16)
    query_weight = noise(keys[4], (D, D), D ** -0.5, 0.15625, ((0, 8),))
    key_weight = noise(keys[5], (D, D), D ** -0.5, 0.15625, ((0, 8),))
    value_weight = noise(keys[6], (D, D), D ** -0.5, 0.15625, ((0, 8),))
    out_weight = noise(keys[7], (D, D), (D // 64) ** -0.5, 1.25, ((0, 8),))
    ffn_gain = jnp.clip(1.0 + 0.18 * jax.random.normal(keys[8], (D,), jnp.float32), 0.099609375, 1.8984375).astype(jnp.bfloat16)
    shared_gate = noise(keys[9], (D, FF), D ** -0.5, 0.15625, ((0, 8),))
    shared_up = noise(keys[10], (D, FF), D ** -0.5, 0.15625, ((0, 8),))
    shared_down = noise(keys[11], (FF, D), FF ** -0.5, 0.1875, ((0, 8),))
    router_weight = noise(keys[12], (D, ROUTED), D ** -0.5, 0.15625, ((0, 8),))
    expert_gate = noise(keys[13], (SLOTS, D, FF), D ** -0.5, 0.15625, ((0, 8),))
    expert_up = noise(keys[14], (SLOTS, D, FF), D ** -0.5, 0.15625, ((0, 8),))
    expert_down = noise(keys[15], (SLOTS, FF, D), (max(1, FF // 256)) ** -0.5, 3.5, ((0, 8),))
    cotangent = noise(keys[16], (SEQS, SEQ, D), 1.0, 6.0, ((0, 32),))
    return {"tokens": tokens, "lengths": lengths, "routes": routes, "attn_gain": attn_gain, "query_weight": query_weight, "key_weight": key_weight, "value_weight": value_weight, "out_weight": out_weight, "ffn_gain": ffn_gain, "shared_gate": shared_gate, "shared_up": shared_up, "shared_down": shared_down, "router_weight": router_weight, "expert_gate": expert_gate, "expert_up": expert_up, "expert_down": expert_down, "cotangent": cotangent}


@jax.custom_vjp
def low(v):
    return lax.optimization_barrier(v.astype(jnp.bfloat16)).astype(jnp.float32)

@jax.custom_vjp
def low_back(v):
    return v

def low_keep(v):
    return (low(v), None)

def low_pass(kept, grad):
    return (grad,)

def back_keep(v):
    return (v, None)

def back_low(kept, grad):
    return (low(grad),)
low.defvjp(low_keep, low_pass)
low_back.defvjp(back_keep, back_low)
epsilon = 1e-06
highest = lax.Precision.HIGHEST

def matmul(left_side, right_side):
    return jnp.dot(left_side, right_side, precision=highest)

def rms_norm(values, gain_vector):
    return values * lax.rsqrt(lax.optimization_barrier(jnp.mean(values * values, axis=-1, keepdims=True)) + epsilon) * gain_vector

def rotary_tables(length):
    halfway = HEAD_DIM // 2
    inverse = 10000.0 ** (-2.0 * jnp.arange(halfway, dtype=jnp.float32) / HEAD_DIM)
    angles = jnp.arange(length, dtype=jnp.float32)[:, None] * inverse[None, :]
    return (jnp.cos(angles)[:, None, :], jnp.sin(angles)[:, None, :])

def rotate(values, cosine_table, sine_table):
    halfway = values.shape[-1] // 2
    first_half = values[..., :halfway]
    second_half = values[..., halfway:]
    return jnp.concatenate([first_half * cosine_table - second_half * sine_table, second_half * cosine_table + first_half * sine_table], axis=-1)

def slot_table(choices):
    flat_ids = choices.reshape(-1).astype(jnp.int32)
    onehot = (flat_ids[:, None] == jnp.arange(SLOTS, dtype=jnp.int32)[None, :]).astype(jnp.int32)
    earlier = jnp.cumsum(onehot, axis=0) - onehot
    places = lax.optimization_barrier(jnp.sum(earlier * onehot, axis=1)).astype(jnp.int32)
    targets = (flat_ids * CAP + places).astype(jnp.int32)
    sources = jnp.full((SLOTS * CAP,), flat_ids.shape[0], jnp.int32)
    sources = sources.at[targets].set(jnp.arange(flat_ids.shape[0], dtype=jnp.int32))
    return (targets, sources)

def pick_rows(table_rows, row_index):
    return table_rows[row_index]

def group_forward(params, inputs, lengths, routes):
    attn_gain, query_weight, key_weight, value_weight, out_weight, ffn_gain, shared_gate, shared_up, shared_down, router_weight, expert_gate, expert_up, expert_down = params
    groups = inputs.shape[0]
    cosine_table, sine_table = rotary_tables(SEQ)
    normed = low(rms_norm(inputs, attn_gain)).reshape(-1, D)

    def project(weight):
        return low_back(matmul(normed, weight)).reshape(groups, SEQ, HEADS, HEAD_DIM)
    queries = low(rotate(project(query_weight), cosine_table, sine_table))
    keys_all = low(rotate(project(key_weight), cosine_table, sine_table))
    values_all = low(project(value_weight))
    scores = low_back(jnp.einsum('gqhd,gkhd->ghqk', queries, keys_all, precision=highest) / math.sqrt(HEAD_DIM))
    positions = jnp.arange(SEQ, dtype=jnp.int32)
    allowed = (positions[None, None, :] <= positions[None, :, None]) & (positions[None, None, :] < lengths[:, None, None])
    scores = jnp.where(allowed[:, None, :, :], scores, -1e+30)
    probabilities = jax.nn.softmax(scores, axis=-1)
    attended = low(low_back(jnp.einsum('ghqk,gkhd->gqhd', low(probabilities), values_all, precision=highest)))
    branch = low_back(matmul(attended.reshape(-1, D), out_weight))
    middle = inputs + branch.reshape(groups, SEQ, D)
    second = low(rms_norm(middle, ffn_gain)).reshape(-1, D)
    shared_hidden = low(jax.nn.silu(low_back(matmul(second, shared_gate))) * low_back(matmul(second, shared_up)))
    shared_out = matmul(shared_hidden, shared_down).reshape(groups, SEQ, D)
    logits = low_back(matmul(second, router_weight))
    gate_probs = jax.nn.softmax(logits, axis=-1).reshape(groups, SEQ, ROUTED)
    chosen = jnp.take_along_axis(gate_probs, routes, axis=2)
    targets, sources = jax.vmap(slot_table)(routes)
    padded = jnp.concatenate([second.reshape(groups, SEQ, D), jnp.zeros((groups, 1, D), second.dtype)], axis=1)
    outgoing = low_back(jax.vmap(pick_rows)(padded, sources // TOP))
    arrived = outgoing.reshape(groups, SLOTS, CAP, D).transpose(1, 0, 2, 3).reshape(SLOTS, groups * CAP, D)
    gate_part = low_back(jnp.einsum('erd,edf->erf', arrived, expert_gate, precision=highest))
    up_part = low_back(jnp.einsum('erd,edf->erf', arrived, expert_up, precision=highest))
    expert_hidden = low(jax.nn.silu(gate_part) * up_part)
    expert_out = low(low_back(jnp.einsum('erf,efd->erd', expert_hidden, expert_down, precision=highest)))
    returned = expert_out.reshape(SLOTS, groups, CAP, D).transpose(1, 0, 2, 3).reshape(groups, SLOTS * CAP, D)
    picked = jax.vmap(pick_rows)(returned, targets).reshape(groups, SEQ, TOP, D)
    routed = lax.optimization_barrier(jnp.sum(picked * chosen[..., None], axis=2))
    return middle + shared_out + routed

def reference(tokens, lengths, routes, attn_gain, query_weight, key_weight, value_weight, out_weight, ffn_gain, shared_gate, shared_up, shared_down, router_weight, expert_gate, expert_up, expert_down, cotangent):
    params = tuple((weight.astype(jnp.float32) for weight in (attn_gain, query_weight, key_weight, value_weight, out_weight, ffn_gain, shared_gate, shared_up, shared_down, router_weight, expert_gate, expert_up, expert_down)))
    blocks = SEQS // 8
    inputs = tokens.astype(jnp.float32).reshape(blocks, 8, SEQ, D)
    length_blocks = lengths.astype(jnp.int32).reshape(blocks, 8)
    route_blocks = routes.astype(jnp.int32).reshape(blocks, 8, SEQ, TOP)

    def forward(weights, block_inputs):
        checked = jax.checkpoint(group_forward)

        def one_block(packed):
            return checked(weights, packed[0], packed[1], packed[2])
        return lax.map(one_block, (block_inputs, length_blocks, route_blocks))
    result, pullback = jax.vjp(forward, params, inputs)
    grad_params, grad_inputs = pullback(cotangent.astype(jnp.float32).reshape(blocks, 8, SEQ, D))
    output = result.reshape(SEQS, SEQ, D).astype(jnp.bfloat16)
    return (output, grad_inputs.reshape(SEQS, SEQ, D), grad_params[0], grad_params[1], grad_params[2], grad_params[3], grad_params[4], grad_params[5], grad_params[6], grad_params[7], grad_params[8], grad_params[9], grad_params[10], grad_params[11], grad_params[12])
```

```python
import math

import jax
import jax.numpy as jnp
from jax import lax
from jax.sharding import PartitionSpec as P

HEAD_DIM = 128
LANES = 128
EPS = 1e-06
LOW = jnp.bfloat16
WIDE = jnp.float32


def dot(a, b, dims=((1,), (0,))):
    return lax.dot_general(a, b, (dims, ((), ())), preferred_element_type=WIDE)


def dot_t(a, b):
    return dot(a, b, ((1,), (1,)))


def dot_rows(a, b):
    return dot(a, b, ((0,), (0,)))


def inverse_rms(v):
    return lax.rsqrt(jnp.mean(v * v, axis=-1, keepdims=True) + EPS)


def rms_back(grad, v, r, gain):
    scaled = grad * gain
    grad_v = r * (scaled - v * (r * r) * jnp.mean(scaled * v, axis=-1, keepdims=True))
    return grad_v, jnp.sum(grad * v * r, axis=0)


def rotary_tables(length):
    halfway = HEAD_DIM // 2
    inverse = 10000.0 ** (-2.0 * jnp.arange(halfway, dtype=WIDE) / HEAD_DIM)
    angles = jnp.arange(length, dtype=WIDE)[:, None] * inverse[None, :]
    return jnp.cos(angles)[:, None, :], jnp.sin(angles)[:, None, :]


def rotate(v, cosine, sine):
    half = v.shape[-1] // 2
    a, b = v[..., :half], v[..., half:]
    return jnp.concatenate([a * cosine - b * sine, b * cosine + a * sine], axis=-1)


def exchange(x, bit):
    count = lax.axis_size("dp")
    return lax.ppermute(x, "dp", [(i, i ^ bit) for i in range(count)])


def dp_bits():
    bits, b = [], 1
    while b < lax.axis_size("dp"):
        bits.append(b)
        b *= 2
    return bits


def dp_sum(x):
    bits = dp_bits()
    cut = x.shape[1] // 2 // LANES * LANES
    parts = []
    for piece, order in ((x[:, :cut], bits), (x[:, cut:], bits[::-1])):
        for bit in order:
            got = exchange(piece, bit)
            piece = (piece.astype(WIDE) + got.astype(WIDE)).astype(LOW)
        parts.append(piece)
    return jnp.concatenate(parts, axis=1)


def dp_scatter(x, order):
    count = lax.axis_size("dp")
    me = lax.axis_index("dp")
    rows = x.shape[0] // count
    x = x.reshape((2,) * len(dp_bits()) + (rows, x.shape[1]))
    axes = {bit: n for n, bit in enumerate(reversed(dp_bits()))}
    left = list(reversed(dp_bits()))
    for bit in order:
        axis = left.index(bit)
        mine = (me // bit) % 2
        kept = lax.dynamic_index_in_dim(x, mine, axis, keepdims=False)
        sent = lax.dynamic_index_in_dim(x, 1 - mine, axis, keepdims=False)
        got = exchange(sent, bit)
        left.remove(bit)
        total = kept.astype(WIDE) + got.astype(WIDE)
        x = total if not left else total.astype(LOW)
    return x


def per_device(
    tokens,
    lengths,
    routes,
    attn_gain,
    query_weight,
    key_weight,
    value_weight,
    out_weight,
    ffn_gain,
    shared_gate,
    shared_up,
    shared_down,
    router_weight,
    expert_gate,
    expert_up,
    expert_down,
    cotangent,
):
    group = lax.axis_size("expert")
    place_of_me = lax.axis_index("expert")
    slot_dev = expert_gate.shape[0]
    slot_count = slot_dev * group
    seq, width = tokens.shape[1:]
    top = routes.shape[2]
    heads = width // HEAD_DIM
    ff = expert_gate.shape[2]
    ff_part = ff // group
    rows_w = width // group
    capacity = max(2, 3 * seq * top // (2 * slot_count))
    cap = -(-capacity // 8) * 8
    routed_count = router_weight.shape[1]

    qkv_local = jnp.concatenate([query_weight, key_weight, value_weight], axis=1)
    qkv = lax.all_gather(qkv_local, "expert", axis=0, tiled=True)
    w_out = lax.all_gather(out_weight, "expert", axis=0, tiled=True)

    small = jnp.concatenate(
        [attn_gain, ffn_gain, router_weight.reshape(-1), routes[0].reshape(-1).astype(LOW)]
    )
    small_all = lax.all_gather(small, "expert", axis=0, tiled=False)
    at = 0
    pieces = []
    for n in (rows_w, rows_w, rows_w * routed_count, seq * top):
        pieces.append(small_all[:, at : at + n])
        at += n
    gain_a = pieces[0].reshape(1, width).astype(WIDE)
    gain_f = pieces[1].reshape(1, width).astype(WIDE)
    router = pieces[2].reshape(width, routed_count)
    routes_all = pieces[3].reshape(group, seq, top).astype(jnp.int32)

    def to_columns(w):
        return w.reshape(w.shape[0], group, ff_part).transpose(1, 0, 2)

    cols_local = jnp.concatenate([to_columns(shared_gate), to_columns(shared_up)], axis=2)
    cols = lax.all_to_all(cols_local, "expert", split_axis=0, concat_axis=0, tiled=True)
    shared_cols = cols.reshape(width, 2 * ff_part)

    inputs = tokens[0].astype(WIDE)
    length_here = lengths[0]
    cosine, sine = rotary_tables(seq)

    r_a = inverse_rms(inputs)
    normed = (inputs * r_a * gain_a).astype(LOW)
    qkv_pre = dot(normed, qkv)
    q_pre = qkv_pre[:, :width].reshape(seq, heads, HEAD_DIM)
    k_pre = qkv_pre[:, width : 2 * width].reshape(seq, heads, HEAD_DIM)
    queries = rotate(q_pre, cosine, sine).astype(LOW)
    keys = rotate(k_pre, cosine, sine).astype(LOW)
    values = qkv_pre[:, 2 * width :].astype(LOW).reshape(seq, heads, HEAD_DIM)
    positions = jnp.arange(seq, dtype=jnp.int32)
    allowed = (positions[None, :] <= positions[:, None]) & (positions[None, :] < length_here)
    root = math.sqrt(HEAD_DIM)
    scores = jnp.einsum("qhd,khd->hqk", queries, keys, preferred_element_type=WIDE) / root
    scores = jnp.where(allowed[None], scores, -1e30)
    probs = jax.nn.softmax(scores, axis=-1)
    probs_low = probs.astype(LOW)
    attended = (
        jnp.einsum("hqk,khd->qhd", probs_low, values, preferred_element_type=WIDE)
        .astype(LOW)
        .reshape(seq, width)
    )
    middle = inputs + dot(attended, w_out)
    r_f = inverse_rms(middle)
    second = (middle * r_f * gain_f).astype(LOW)

    incoming = cotangent[0]
    second_all = lax.all_gather(second, "expert", axis=0, tiled=True)
    up_all = lax.all_gather(incoming, "expert", axis=0, tiled=True)

    my_slots = place_of_me * slot_dev + jnp.arange(slot_dev, dtype=jnp.int32)
    member = jnp.any(
        routes_all[None] == my_slots[:, None, None, None], axis=-1
    )
    earlier = (positions[:, None] < positions[None, :]).astype(LOW)
    place = jnp.einsum("egb,bt->egt", member.astype(LOW), earlier, preferred_element_type=WIDE)
    place = place.astype(jnp.int32)
    hit = (place[:, :, None, :] == jnp.arange(cap, dtype=jnp.int32)[None, None, :, None]) & (
        member[:, :, None, :]
    )
    pick = hit.astype(LOW)

    logits_all = dot(second_all, router)
    probs_all = jax.nn.softmax(logits_all, axis=-1).reshape(group, seq, routed_count)
    chosen_all = jnp.sum(
        jnp.where(
            jnp.arange(routed_count, dtype=jnp.int32)[None, None, None, :]
            == my_slots[:, None, None, None],
            probs_all[None],
            0.0,
        ),
        axis=-1,
    )
    chosen_rows = jnp.sum(jnp.where(hit, chosen_all[:, :, None, :], 0.0), axis=-1)
    chosen_rows = chosen_rows.reshape(slot_dev, group * cap, 1)

    def to_slots(x):
        x = x.reshape(group, seq, width)
        out = jnp.einsum("egct,gtd->egcd", pick, x, preferred_element_type=WIDE).astype(LOW)
        return out.reshape(slot_dev, group * cap, width)

    def to_tokens(x):
        x = x.reshape(slot_dev, group, cap, width)
        out = jnp.einsum("egct,egcd->gtd", pick, x, preferred_element_type=WIDE)
        return out.reshape(group * seq, width)

    def per_slot(spec, a, b):
        return jnp.einsum(spec, a, b, preferred_element_type=WIDE)

    rows = to_slots(second_all)
    gate = per_slot("erd,edf->erf", rows, expert_gate)
    up = per_slot("erd,edf->erf", rows, expert_up)
    sig = jax.nn.sigmoid(gate)
    silu = gate * sig
    hidden = (silu * up).astype(LOW)
    expert_out = per_slot("erf,efd->erd", hidden, expert_down).astype(LOW)

    sh = dot(second_all, shared_cols)
    s_gate, s_up = sh[:, :ff_part], sh[:, ff_part:]
    s_sig = jax.nn.sigmoid(s_gate)
    s_silu = s_gate * s_sig
    s_hidden = (s_silu * s_up).astype(LOW)

    weighted = (expert_out.astype(WIDE) * chosen_rows).astype(LOW)
    forward_part = (to_tokens(weighted) + dot(s_hidden, shared_down)).astype(LOW)
    forward_sum = lax.psum_scatter(forward_part, "expert", scatter_dimension=0, tiled=True)
    output = (middle + forward_sum.astype(WIDE)).astype(LOW)

    g_rows_up = to_slots(up_all)
    g_choice_rows = jnp.sum(g_rows_up.astype(WIDE) * expert_out.astype(WIDE), axis=-1)
    g_expert_out = (chosen_rows * g_rows_up.astype(WIDE)).astype(LOW)
    g_hidden = per_slot("erd,efd->erf", g_expert_out, expert_down)
    g_gate = (g_hidden * up * (sig * (1.0 + gate * (1.0 - sig)))).astype(LOW)
    g_up = (g_hidden * silu).astype(LOW)
    g_rows = (
        per_slot("erf,edf->erd", g_gate, expert_gate) + per_slot("erf,edf->erd", g_up, expert_up)
    ).astype(LOW)

    g_s_hidden = dot_t(up_all, shared_down)
    g_s_gate = (g_s_hidden * s_up * (s_sig * (1.0 + s_gate * (1.0 - s_sig)))).astype(LOW)
    g_s_up = (g_s_hidden * s_silu).astype(LOW)
    g_s = jnp.concatenate([g_s_gate, g_s_up], axis=1)

    g_choice = jnp.einsum(
        "egct,egc->egt",
        hit.astype(WIDE),
        g_choice_rows.reshape(slot_dev, group, cap),
        precision=lax.Precision.HIGHEST,
    )
    lane = jnp.arange(LANES, dtype=jnp.int32)
    spread = jnp.zeros((group, seq, 2 * slot_count), WIDE)
    columns = jnp.arange(2 * slot_count, dtype=jnp.int32)
    high = g_choice.astype(LOW).astype(WIDE)
    rest = g_choice - high
    for n in range(slot_dev):
        spread = spread + jnp.where(columns == my_slots[n], high[n][..., None], 0.0)
        spread = spread + jnp.where(columns == my_slots[n] + slot_count, rest[n][..., None], 0.0)
    spread = spread.reshape(group * seq, 2 * slot_count).astype(LOW)
    spread = jnp.pad(spread, ((0, 0), (0, -(2 * slot_count) % LANES)))
    back_part = (to_tokens(g_rows) + dot_t(g_s, shared_cols)).astype(LOW)
    back_part = jnp.concatenate([back_part, spread], axis=1)
    back_sum = lax.psum_scatter(back_part, "expert", scatter_dimension=0, tiled=True)

    def scattered(a, b):
        out = []
        for n in range(slot_dev):
            g = dot_rows(a[n], b[n]).astype(LOW)
            bits = dp_bits()
            out.append(dp_scatter(g, bits if n % 2 == 0 else bits[::-1]))
        return jnp.stack(out)

    grad_down = scattered(hidden, g_expert_out)
    grad_gate = scattered(rows, g_gate)
    grad_up = scattered(rows, g_up)

    g_cols = dot_rows(second_all, g_s).astype(LOW)
    grad_sdown = dot_rows(s_hidden, up_all).astype(LOW)
    g_cols = lax.all_to_all(
        g_cols.reshape(group, rows_w, 2 * ff_part), "expert", split_axis=0, concat_axis=0, tiled=True
    )
    g_cols = g_cols.transpose(1, 0, 2)
    grad_sgate = g_cols[:, :, :ff_part].reshape(rows_w, ff)
    grad_sup = g_cols[:, :, ff_part:].reshape(rows_w, ff)
    shared_sum = dp_sum(jnp.concatenate([grad_sgate, grad_sup], axis=1))
    sdown_sum = dp_sum(grad_sdown)

    upstream = incoming.astype(WIDE)
    logits = dot(second, router)
    gate_probs = jax.nn.softmax(logits, axis=-1)
    g_gates = (
        back_sum[:, width : width + routed_count].astype(WIDE)
        + back_sum[:, width + slot_count : width + slot_count + routed_count].astype(WIDE)
    )
    g_logits = gate_probs * (g_gates - jnp.sum(g_gates * gate_probs, axis=-1, keepdims=True))
    g_logits = g_logits.astype(LOW)
    grad_router = dot_rows(second, g_logits)
    g_second = back_sum[:, :width].astype(WIDE) + dot_t(g_logits, router)
    g_norm, grad_ffn_gain = rms_back(g_second, middle, r_f, gain_f)
    g_middle = upstream + g_norm
    g_middle_low = g_middle.astype(LOW)
    grad_out = dot_rows(attended, g_middle_low)
    extra = jnp.concatenate([grad_router, grad_ffn_gain[:, None]], axis=1)
    extra = jnp.pad(extra, ((0, 0), (0, -(routed_count + 1) % LANES)))
    first_sum = dp_sum(
        lax.psum_scatter(
            jnp.concatenate([grad_out.astype(LOW), extra.astype(LOW)], axis=1),
            "expert",
            scatter_dimension=0,
            tiled=True,
        )
    )

    g_attended = dot_t(g_middle_low, w_out).astype(LOW).reshape(seq, heads, HEAD_DIM)
    g_probs = jnp.einsum("qhd,khd->hqk", g_attended, values, preferred_element_type=WIDE)
    g_values = jnp.einsum("hqk,qhd->khd", probs_low, g_attended, preferred_element_type=WIDE)
    g_scores = (probs * (g_probs - jnp.sum(g_probs * probs, axis=-1, keepdims=True))).astype(LOW)
    g_q = jnp.einsum("hqk,khd->qhd", g_scores, keys, preferred_element_type=WIDE) / root
    g_k = jnp.einsum("hqk,qhd->khd", g_scores, queries, preferred_element_type=WIDE) / root
    g_q = rotate(g_q, cosine, -sine).astype(LOW).reshape(seq, width)
    g_k = rotate(g_k, cosine, -sine).astype(LOW).reshape(seq, width)
    g_v = g_values.astype(LOW).reshape(seq, width)
    g_qkv = jnp.concatenate([g_q, g_k, g_v], axis=1)
    grad_qkv = dot_rows(normed, g_qkv)
    g_normed = dot_t(g_qkv, qkv)
    g_inputs, grad_attn_gain = rms_back(g_normed, inputs, r_a, gain_a)
    grad_tokens = g_middle + g_inputs
    extra = jnp.pad(grad_attn_gain[:, None], ((0, 0), (0, LANES - 1)))
    second_sum = dp_sum(
        lax.psum_scatter(
            jnp.concatenate([grad_qkv.astype(LOW), extra.astype(LOW)], axis=1),
            "expert",
            scatter_dimension=0,
            tiled=True,
        )
    )

    def wide(x):
        return x.astype(WIDE)

    return (
        output[None],
        grad_tokens[None],
        wide(second_sum[:, 3 * width]),
        wide(second_sum[:, :width]),
        wide(second_sum[:, width : 2 * width]),
        wide(second_sum[:, 2 * width : 3 * width]),
        wide(first_sum[:, :width]),
        wide(first_sum[:, width + routed_count]),
        wide(shared_sum[:, :ff]),
        wide(shared_sum[:, ff:]),
        wide(sdown_sum),
        wide(first_sum[:, width : width + routed_count]),
        wide(grad_gate),
        wide(grad_up),
        wide(grad_down),
    )


def solution(mesh):
    split = ("dp", "expert")
    e1, e2, e3 = P("expert"), P("expert", None), P("expert", None, None)
    s3 = P(split, None, None)
    scattered = P("expert", "dp", None)
    return jax.shard_map(
        per_device,
        mesh=mesh,
        in_specs=(s3, P(split), s3, e1, e2, e2, e2, e2, e1, e2, e2, e2, e2, e3, e3, e3, s3),
        out_specs=(s3, s3, e1, e2, e2, e2, e2, e1, e2, e2, e2, e2) + (scattered,) * 3,
        check_vma=False,
    )
```

```python
import functools
import math

import jax
import jax.numpy as jnp
from jax import lax
from jax.experimental import pallas as pl
from jax.experimental.pallas import tpu as pltpu
from jax.sharding import PartitionSpec as P


HEAD_DIM = 128
LANES = 128
EPS = 1e-06
LOW = jnp.bfloat16
WIDE = jnp.float32
INT = jnp.int32


def dot(a, b, dims=((1,), (0,))):
    return lax.dot_general(a, b, (dims, ((), ())), preferred_element_type=WIDE)


def dot_t(a, b):
    return dot(a, b, ((1,), (1,)))


def dot_rows(a, b):
    return dot(a, b, ((0,), (0,)))


def inverse_rms(v):
    return lax.rsqrt(jnp.mean(v * v, axis=-1, keepdims=True) + EPS)


def iota(shape, axis):
    return lax.broadcasted_iota(INT, shape, axis)


def lane_pick(x, lane):
    return jnp.sum(jnp.where(iota(x.shape, 1) == lane, x, jnp.zeros_like(x)), axis=1, keepdims=True)


def masked_softmax(logits, count):
    logits = jnp.where(iota(logits.shape, 1) < count, logits, -1e30)
    e = jnp.exp(logits - jnp.max(logits, axis=-1, keepdims=True))
    return e / jnp.sum(e, axis=-1, keepdims=True)


def whole(shape):
    n = len(shape)
    return pl.BlockSpec(shape, lambda *_: (0,) * n, pipeline_mode=pl.Buffered(1))


def cost(flops, size):
    return pl.CostEstimate(flops=int(flops), bytes_accessed=int(size), transcendentals=0)


def turn(v, cosine, sine):
    return v * cosine + pltpu.roll(v, HEAD_DIM // 2, 1) * sine


def head_probs(q, k, allowed):
    s = dot_t(q, k) * (1.0 / math.sqrt(HEAD_DIM))
    s = jnp.where(allowed, s, -1e30)
    e = jnp.exp(s - jnp.max(s, axis=-1, keepdims=True))
    return e * (1.0 / jnp.sum(e, axis=-1, keepdims=True))


def allowed_keys(seq, length):
    key = iota((seq, seq), 1)
    return (key <= iota((seq, seq), 0)) & (key < length)


def attend_kernel(
    pair, length_ref, x_ref, gain_ref, cos_ref, sin_ref, wq_ref, wk_ref, wv_ref, qkv_ref, out_ref, normed
):
    seq = x_ref.shape[0]
    part = pair * HEAD_DIM

    @pl.when(pl.program_id(0) == 0)
    def _():
        x = x_ref[...].astype(WIDE)
        normed[...] = (x * inverse_rms(x) * gain_ref[...]).astype(LOW)

    pre_q, pre_k, pre_v = (dot(normed[...], w[...]) for w in (wq_ref, wk_ref, wv_ref))
    allowed = allowed_keys(seq, length_ref[0])
    cosine, sine = cos_ref[...], sin_ref[...]
    for i in range(pair):
        at = i * HEAD_DIM
        q = turn(pre_q[:, at : at + HEAD_DIM], cosine, sine).astype(LOW)
        k = turn(pre_k[:, at : at + HEAD_DIM], cosine, sine).astype(LOW)
        v = pre_v[:, at : at + HEAD_DIM].astype(LOW)
        qkv_ref[:, at : at + HEAD_DIM] = q
        qkv_ref[:, part + at : part + at + HEAD_DIM] = k
        qkv_ref[:, 2 * part + at : 2 * part + at + HEAD_DIM] = v
        p = head_probs(q, k, allowed).astype(LOW)
        out_ref[:, at : at + HEAD_DIM] = dot(p, v).astype(LOW)


def assemble_kernel(rows_ref, columns_ref, *refs):
    *pieces, out_ref, sems = refs
    copies = []
    for n, piece in enumerate(pieces):
        r, c = piece.shape
        place = out_ref.at[
            pl.ds(pl.multiple_of(rows_ref[n] * r, r), r), pl.ds(pl.multiple_of(columns_ref[n] * c, c), c)
        ]
        copies.append(pltpu.make_async_copy(piece, place, sems.at[n]))
    for copy in copies:
        copy.start()
    for copy in copies:
        copy.wait()


def project_kernel(att_ref, w_ref, x_ref, gain_ref, middle_ref, second_ref):
    middle = x_ref[...].astype(WIDE) + dot(att_ref[...], w_ref[...])
    middle_ref[...] = middle
    second_ref[...] = (middle * inverse_rms(middle) * gain_ref[...]).astype(LOW)


def middle_kernel(
    routed, slots, back_ref, second_ref, router_ref, middle_ref, gain_ref, up_ref, att_ref,
    wide_ref, low_ref, grads_ref,
):
    width = middle_ref.shape[1]
    second, router = second_ref[...], router_ref[...]
    probs = masked_softmax(dot(second, router), routed)
    both = back_ref[:, width:]
    lane = iota(both.shape, 1)
    g_gates = jnp.where(lane < routed, both + pltpu.roll(both, LANES - slots, 1), 0.0)
    g_logits = probs * (g_gates - jnp.sum(g_gates * probs, axis=-1, keepdims=True))
    g_logits = g_logits.astype(LOW)
    g_second = back_ref[:, :width] + dot_t(g_logits, router)
    middle = middle_ref[...]
    r = inverse_rms(middle)
    scaled = g_second * gain_ref[...]
    g_norm = r * (scaled - middle * (r * r) * jnp.mean(scaled * middle, axis=-1, keepdims=True))
    g_middle = up_ref[...].astype(WIDE) + g_norm
    wide_ref[...] = g_middle
    low = g_middle.astype(LOW)
    low_ref[...] = low
    grads_ref[:, :width] = dot_rows(att_ref[...], low).astype(LOW)
    g_gain = jnp.sum(g_second * middle * r, axis=0, keepdims=True)
    first = jnp.where(iota((8, width), 0) == 0, jnp.broadcast_to(g_gain, (8, width)), 0.0)
    mark = ((iota((8, LANES), 0) == 0) & (iota((8, LANES), 1) == routed)).astype(LOW)
    grads_ref[:, width:] = (dot_rows(second, g_logits) + dot_rows(first.astype(LOW), mark)).astype(LOW)


def attend_back_kernel(
    pair, length_ref, low_ref, wide_ref, x_ref, gain_ref, cos_ref, sin_ref, qkv_ref, wq_ref, wk_ref, wv_ref,
    wo_ref, tokens_ref, grads_ref, normed, total, ready, gain_ready, sems,
):
    seq, width = x_ref.shape
    part = pair * HEAD_DIM
    step = pl.program_id(0)
    steps = pl.num_programs(0)
    slot = lax.rem(step, 2)

    def leave(n, at):
        copies = []
        for i in range(3):
            columns = pl.ds(pl.multiple_of(i * width + n * part, LANES), part)
            copies.append(
                pltpu.make_async_copy(ready.at[at, i], grads_ref.at[:, columns], sems.at[at, i])
            )
        return copies

    @pl.when(step == 0)
    def _():
        x = x_ref[...].astype(WIDE)
        normed[...] = (x * inverse_rms(x) * gain_ref[...]).astype(LOW)
        total[...] = jnp.zeros_like(total)

    allowed = allowed_keys(seq, length_ref[0])
    cosine, sine = cos_ref[...], sin_ref[...]
    g_att = dot_t(low_ref[...], wo_ref[...]).astype(LOW)
    root = 1.0 / math.sqrt(HEAD_DIM)
    gq, gk, gv = [], [], []
    for i in range(pair):
        at = i * HEAD_DIM
        q = qkv_ref[:, at : at + HEAD_DIM]
        k = qkv_ref[:, part + at : part + at + HEAD_DIM]
        v = qkv_ref[:, 2 * part + at : 2 * part + at + HEAD_DIM]
        ga = g_att[:, at : at + HEAD_DIM]
        p = head_probs(q, k, allowed)
        gp = dot_t(ga, v)
        gv.append(dot_rows(p.astype(LOW), ga))
        ds = (p * (gp - jnp.sum(gp * p, axis=-1, keepdims=True))).astype(LOW)
        gq.append(turn(dot(ds, k) * root, cosine, -sine))
        gk.append(turn(dot_rows(ds, q) * root, cosine, -sine))
    g = jnp.concatenate(gq + gk + gv, axis=1).astype(LOW)

    @pl.when(step >= 2)
    def _():
        for copy in leave(step - 2, slot):
            copy.wait()

    for i, w_ref in enumerate((wq_ref, wk_ref, wv_ref)):
        piece = g[:, i * part : (i + 1) * part]
        total[...] += dot_t(piece, w_ref[...])
        ready[slot, i] = dot_rows(normed[...], piece).astype(LOW)
    for copy in leave(step, slot):
        copy.start()

    @pl.when(step == steps - 1)
    def _():
        x = x_ref[...].astype(WIDE)
        r = inverse_rms(x)
        grad = total[...]
        scaled = grad * gain_ref[...]
        back = r * (scaled - x * (r * r) * jnp.mean(scaled * x, axis=-1, keepdims=True))
        tokens_ref[...] = wide_ref[...] + back
        g_gain = jnp.sum(grad * x * r, axis=0, keepdims=True)
        first = jnp.where(iota((8, width), 0) == 0, jnp.broadcast_to(g_gain, (8, width)), 0.0)
        mark = ((iota((8, LANES), 0) == 0) & (iota((8, LANES), 1) == 0)).astype(LOW)
        gain_ready[...] = dot_rows(first.astype(LOW), mark).astype(LOW)
        last = pltpu.make_async_copy(gain_ready, grads_ref.at[:, 3 * width :], sems.at[2, 0])
        last.start()
        for copy in leave(step - 1, 1 - slot) + leave(step, slot) + [last]:
            copy.wait()


def silu_parts(gate):
    sig = 1.0 / (1.0 + jnp.exp(-gate))
    return gate * sig, sig * (1.0 + gate * (1.0 - sig))


def slots_of(hits, blocks):
    return jnp.concatenate([dot(h, x) for h, x in zip(hits, blocks)], axis=0).astype(LOW)


def row_hits(prow_ref, cap):
    count, _, seq = prow_ref.shape[1:]
    return [
        (iota((cap, seq), 0) == prow_ref[0, i]).astype(WIDE).astype(LOW) for i in range(count)
    ]


def column_hit(pcol_ref, at, e, cap):
    place = lane_pick(pcol_ref[at, :], e)
    return (iota((at.stop - at.start, cap), 1) == place).astype(WIDE).astype(LOW)


def experts_kernel(
    routed, slots_ref, s0_ref, s1_ref, prow_ref, pcol_ref, router_ref, wgu_ref, wd_ref, sc_ref, sd_ref,
    *refs,
):
    (rows_ref, hid_ref, sh_ref, sec_ref, a_ref, b_ref, picked_ref, probs_ref, sa_ref, sb_ref,
     part0_ref, part1_ref, total) = refs[-13:]
    seq, _ = s0_ref.shape
    cap = rows_ref.shape[2] // 2
    ff = wd_ref.shape[1]
    fp = sd_ref.shape[0]
    e = pl.program_id(0)

    @pl.when(e == 0)
    def _():
        sec_ref[0, :seq] = s0_ref[...]
        sec_ref[0, seq:] = s1_ref[...]
        probs_ref[...] = masked_softmax(dot(sec_ref[0], router_ref[...]), routed)
        mid = dot(sec_ref[0], sc_ref[...])
        silu, slope = silu_parts(mid[:, :fp])
        up = mid[:, fp:]
        hidden = (silu * up).astype(LOW)
        sa_ref[...] = silu.astype(LOW)
        sb_ref[...] = (up * slope).astype(LOW)
        sh_ref[0] = hidden
        total[...] = dot(hidden, sd_ref[...])

    slot = slots_ref[e]
    x = slots_of(row_hits(prow_ref, cap), (s0_ref[...], s1_ref[...]))
    rows_ref[0, 0] = x
    mid = dot(x, wgu_ref[0])
    silu, slope = silu_parts(mid[:, :ff])
    up = mid[:, ff:]
    hidden = (silu * up).astype(LOW)
    a_ref[0] = silu.astype(LOW)
    b_ref[0] = (up * slope).astype(LOW)
    hid_ref[0, 0] = hidden
    out = dot(hidden, wd_ref[0])
    for i in range(2):
        at = slice(i * seq, (i + 1) * seq)
        picked = dot(column_hit(pcol_ref, at, e, cap), out[i * cap : (i + 1) * cap].astype(LOW))
        picked_ref[0, at] = picked.astype(LOW)
        total[at, :] += lane_pick(probs_ref[at, :], slot) * picked

    @pl.when(e == pl.num_programs(0) - 1)
    def _():
        part0_ref[...] = total[:seq].astype(LOW)
        part1_ref[...] = total[seq:].astype(LOW)


def experts_back_kernel(
    slot_count, slots_ref, g0_ref, g1_ref, prow_ref, pcol_ref, probs_ref, picked_ref, a_ref, b_ref,
    wgu_ref, wd_ref, sc_ref, sd_ref, sa_ref, sb_ref, *refs,
):
    grows_ref, ggu_ref, gs_ref, up_ref, back0_ref, back1_ref, total, extra = refs[-8:]
    seq, width = g0_ref.shape
    cap = grows_ref.shape[2] // 2
    e = pl.program_id(0)

    @pl.when(e == 0)
    def _():
        up_ref[0, :seq] = g0_ref[...]
        up_ref[0, seq:] = g1_ref[...]
        gh = dot_t(up_ref[0], sd_ref[...])
        gs = jnp.concatenate([gh * sb_ref[...].astype(WIDE), gh * sa_ref[...].astype(WIDE)], axis=1)
        gs = gs.astype(LOW)
        gs_ref[0] = gs
        total[...] = dot_t(gs, sc_ref[...])
        extra[...] = jnp.zeros_like(extra)

    slot = slots_ref[e]
    scaled = []
    for i, g_ref in enumerate((g0_ref, g1_ref)):
        at = slice(i * seq, (i + 1) * seq)
        up = g_ref[...].astype(WIDE)
        scaled.append((lane_pick(probs_ref[at, :], slot) * up).astype(LOW))
        choice = jnp.sum(up * picked_ref[0, at].astype(WIDE), axis=1, keepdims=True)
        high = choice.astype(LOW).astype(WIDE)
        lane = iota((seq, LANES), 1)
        extra[at, :] += jnp.where(
            lane == slot, high, jnp.where(lane == slot + slot_count, choice - high, 0.0)
        )
    x = slots_of(row_hits(prow_ref, cap), scaled)
    grows_ref[0, 0] = x
    gh = dot_t(x, wd_ref[0])
    g = jnp.concatenate([gh * b_ref[0].astype(WIDE), gh * a_ref[0].astype(WIDE)], axis=1)
    g = g.astype(LOW)
    ggu_ref[0, 0] = g
    out = dot_t(g, wgu_ref[0])
    for i in range(2):
        at = slice(i * seq, (i + 1) * seq)
        total[at, :] += dot(column_hit(pcol_ref, at, e, cap), out[i * cap : (i + 1) * cap].astype(LOW))

    @pl.when(e == pl.num_programs(0) - 1)
    def _():
        for i, ref in enumerate((back0_ref, back1_ref)):
            at = slice(i * seq, (i + 1) * seq)
            ref[:, :width] = total[at, :].astype(LOW)
            ref[:, width:] = extra[at, :].astype(LOW)


def around(x):
    count = lax.axis_size("expert")
    return lax.ppermute(x, "expert", [(i, (i + 2) % count) for i in range(count)])


def partner(x):
    count = lax.axis_size("expert")
    return lax.ppermute(x, "expert", [(i, i ^ 1) for i in range(count)])


def add(*xs):
    return sum(x.astype(WIDE) for x in xs)


def ring_gather(x, behind=None):
    blocks = []
    for k in range(lax.axis_size("expert") // 2):
        if k == 2 and behind:
            x, _ = after_that(x, behind[-1][0])
        if k:
            x = around(x)
        blocks.append((x, partner(x)))
    return blocks


def ring_sum(parts):
    chips = len(parts)
    total = None
    for k in [*range(1, chips), 0]:
        mine = (parts[k][0], partner(parts[k][1]))
        if total is None:
            total = add(*mine)
        else:
            total = around(total.astype(LOW))
            total = add(*mine, total)
    return total


def exchange(x, bit):
    count = lax.axis_size("dp")
    return lax.ppermute(x, "dp", [(i, i ^ bit) for i in range(count)])


def dp_bits():
    bits, b = [], 1
    while b < lax.axis_size("dp"):
        bits.append(b)
        b *= 2
    return bits


def dp_sum(x):
    bits = dp_bits()
    cut = x.shape[1] // 2 // LANES * LANES
    parts = []
    for piece, order in ((x[:, :cut], bits), (x[:, cut:], bits[::-1])):
        for bit in order:
            got = exchange(piece, bit)
            piece = (piece.astype(WIDE) + got.astype(WIDE)).astype(LOW)
        parts.append(piece)
    return jnp.concatenate(parts, axis=1)


def dp_scatter(x, order, axis=0):
    me = lax.axis_index("dp")
    left = list(reversed(dp_bits()))
    lead, tail = x.shape[:axis], x.shape[axis + 1 :]
    x = x.reshape(*lead, *(2 for _ in left), x.shape[axis] // lax.axis_size("dp"), *tail)
    for bit in order:
        at = axis + left.index(bit)
        mine = (me // bit) % 2
        kept = lax.dynamic_index_in_dim(x, mine, at, keepdims=False)
        sent = lax.dynamic_index_in_dim(x, 1 - mine, at, keepdims=False)
        got = exchange(sent, bit)
        left.remove(bit)
        total = kept.astype(WIDE) + got.astype(WIDE)
        x = total if not left else total.astype(LOW)
    return x


def after_that(x, needed):
    return lax.optimization_barrier((x, needed))


def per_device(
    tokens,
    lengths,
    routes,
    attn_gain,
    query_weight,
    key_weight,
    value_weight,
    out_weight,
    ffn_gain,
    shared_gate,
    shared_up,
    shared_down,
    router_weight,
    expert_gate,
    expert_up,
    expert_down,
    cotangent,
):
    group = lax.axis_size("expert")
    place_of_me = lax.axis_index("expert")
    local = expert_gate.shape[0]
    slot_count = local * group
    seq, width = tokens.shape[1:]
    top = routes.shape[2]
    heads = width // HEAD_DIM
    ff = expert_gate.shape[2]
    ff_part = ff // group
    fp = -(-ff_part // LANES) * LANES
    rows_w = width // group
    capacity = max(2, 3 * seq * top // (2 * slot_count))
    cap = -(-capacity // 8) * 8
    routed = router_weight.shape[1]
    pair = 2
    steps = heads // pair
    part = pair * HEAD_DIM
    shape = jax.ShapeDtypeStruct

    count = lax.axis_size("dp")
    dp = lax.axis_index("dp")
    vo_local = jnp.concatenate([value_weight, out_weight], axis=1)
    strip = 2 * width // count
    vo_part = lax.all_gather(
        lax.dynamic_slice_in_dim(vo_local, dp * strip, strip, 1), "expert", axis=0, tiled=True
    )
    qk = jnp.concatenate([query_weight, key_weight], axis=1)
    qk = lax.all_gather(qk, "expert", axis=0, tiled=True)
    half = width // 2
    core = place_of_me % 2
    pieces = [lax.dynamic_slice_in_dim(vo_part, core * half, half, 0)]
    for bit in dp_bits():
        pieces += [exchange(p, bit) for p in pieces]
    placed = [(p, core ^ other, dp ^ n) for n, piece in enumerate(pieces)
              for other, p in enumerate((piece, partner(piece)))]
    smem = pl.BlockSpec(memory_space=pltpu.SMEM)
    vo = pl.pallas_call(
        assemble_kernel,
        in_specs=[smem, smem] + [pl.BlockSpec(memory_space=pltpu.VMEM)] * len(placed),
        out_specs=pl.BlockSpec(memory_space=pl.ANY),
        out_shape=shape((width, 2 * width), LOW),
        scratch_shapes=[pltpu.SemaphoreType.DMA((len(placed),))],
        cost_estimate=cost(0, 8 * width * width),
        name="assemble",
    )(jnp.stack([p[1] for p in placed]), jnp.stack([p[2] for p in placed]), *(p[0] for p in placed))

    small = jnp.concatenate(
        [attn_gain, ffn_gain, router_weight.reshape(-1), routes[0].reshape(-1).astype(LOW)]
    )
    length_small = small.shape[0]
    small = jnp.pad(small, (0, -length_small % LANES)).reshape(-1, LANES)
    small_all = lax.all_gather(small, "expert", axis=0, tiled=True).reshape(group, -1)
    at = 0
    pieces = []
    for n in (rows_w, rows_w, rows_w * routed, seq * top):
        pieces.append(small_all[:, at : at + n])
        at += n
    gain_a = pieces[0].reshape(1, width).astype(WIDE)
    gain_f = pieces[1].reshape(1, width).astype(WIDE)
    router = jnp.pad(pieces[2].reshape(width, routed), ((0, 0), (0, LANES - routed)))
    routes_all = pieces[3].reshape(group, seq, top).astype(INT)
    chips = group // 2
    back = jnp.arange(chips, dtype=INT)[:, None]
    met = 2 * ((place_of_me // 2 - back) % chips) + (core ^ jnp.arange(2, dtype=INT)[None, :])
    routes_all = routes_all[met.reshape(-1)]

    def to_columns(w):
        w = w.reshape(w.shape[0], group, ff_part).transpose(1, 0, 2)
        return jnp.pad(w, ((0, 0), (0, 0), (0, fp - ff_part)))

    def trim(x):
        return x[..., :ff_part]

    cols_local = jnp.concatenate([to_columns(shared_gate), to_columns(shared_up)], axis=2)
    cols = lax.all_to_all(cols_local, "expert", split_axis=0, concat_axis=0, tiled=True)
    shared_cols = cols.reshape(width, 2 * fp)
    shared_rows = jnp.pad(shared_down, ((0, fp - ff_part), (0, 0)))
    w_gu = jnp.concatenate([expert_gate, expert_up], axis=2)

    my_slots = place_of_me * local + jnp.arange(local, dtype=INT)
    positions = jnp.arange(seq, dtype=INT)
    member = jnp.any(routes_all[None] == my_slots[:, None, None, None], axis=-1)
    earlier = (positions[:, None] < positions[None, :]).astype(LOW)
    place = jnp.einsum("egb,bt->egt", member.astype(LOW), earlier, preferred_element_type=WIDE)
    place = jnp.where(member, place.astype(INT), -1)
    place_row = place[:, :, None, :]
    place_col = jnp.pad(
        place.reshape(local, group * seq).T, ((0, 0), (0, LANES - local)), constant_values=-1
    )

    halfway = HEAD_DIM // 2
    inverse = 10000.0 ** (-2.0 * jnp.arange(halfway, dtype=WIDE) / HEAD_DIM)
    angles = jnp.arange(seq, dtype=WIDE)[:, None] * inverse[None, :]
    cosine = jnp.tile(jnp.cos(angles), (1, 2))
    sine = jnp.concatenate([-jnp.sin(angles), jnp.sin(angles)], axis=1)

    x_low = tokens[0]
    incoming = cotangent[0]
    early = (shared_cols, shared_rows, w_gu, place_row, place_col, router)
    qk, early = after_that(qk, early)
    incoming, qk = after_that(incoming, qk)
    shared_cols, shared_rows, w_gu, place_row, place_col, router = early

    def columns(n):
        return pl.BlockSpec((seq, n), lambda h: (0, h))

    qkv_specs = [pl.BlockSpec((width, part), lambda h: (0, h)),
                 pl.BlockSpec((width, part), lambda h: (0, steps + h)),
                 pl.BlockSpec((width, part), lambda h: (0, h))]

    saved, attended = pl.pallas_call(
        functools.partial(attend_kernel, pair),
        grid=(steps,),
        in_specs=[smem, whole((seq, width)), whole((1, width)), whole((seq, HEAD_DIM)),
                  whole((seq, HEAD_DIM)), *qkv_specs],
        out_specs=[columns(3 * part), columns(part)],
        out_shape=[shape((seq, 3 * width), LOW), shape((seq, width), LOW)],
        scratch_shapes=[pltpu.VMEM((seq, width), LOW)],
        cost_estimate=cost(2 * seq * width * 3 * width * 1.3, 6 * width * width),
        name="attend",
    )(lengths, x_low, gain_a, cosine, sine, qk, qk, vo)
    middle, second = pl.pallas_call(
        project_kernel,
        grid=(1,),
        in_specs=[whole((seq, width)), pl.BlockSpec((width, width), lambda _: (0, 1)),
                  whole((seq, width)), whole((1, width))],
        out_specs=[whole((seq, width)), whole((seq, width))],
        out_shape=[shape((seq, width), WIDE), shape((seq, width), LOW)],
        cost_estimate=cost(2 * seq * width * width, 4 * width * width),
        name="project",
    )(attended, vo, x_low, gain_f)

    anywhere = pl.BlockSpec(memory_space=pl.ANY)
    tok, row = 2 * seq, 2 * cap
    flops = 2 * local * row * 3 * width * ff
    weights = (w_gu, expert_down, shared_cols, shared_rows)
    weight_specs = [pl.BlockSpec((1, width, 2 * ff), lambda e: (e, 0, 0)),
                    pl.BlockSpec((1, ff, width), lambda e: (e, 0, 0)),
                    whole((width, 2 * fp)), whole((fp, width))]

    def low(*dims):
        return shape(dims, LOW)

    def per_slot(k, r, n):
        return pl.BlockSpec((1, 1, r, n), lambda e: (e, k, 0, 0))

    def per_chip(k, r, n):
        return pl.BlockSpec((1, r, n), lambda e: (k, 0, 0))

    def by_slot(r, n):
        return pl.BlockSpec((1, r, n), lambda e: (e, 0, 0))

    def place_specs(k):
        return [pl.BlockSpec((1, 2, 1, seq), lambda e: (e, k, 0, 0)),
                pl.BlockSpec((tok, LANES), lambda e: (k, 0))]

    kept, parts = [], []
    store = ()
    blocks = ring_gather(second)
    for k in range(chips):
        store_in = [anywhere] * len(store)
        fixed = (my_slots, *blocks[k], place_row, place_col, router, *weights)
        out = pl.pallas_call(
            functools.partial(experts_kernel, routed),
            grid=(local,),
            in_specs=[smem, whole((seq, width)), whole((seq, width)), *place_specs(k),
                      whole((width, LANES)), *weight_specs, *store_in],
            out_specs=[per_slot(k, row, width), per_slot(k, row, ff), per_chip(k, tok, fp),
                       per_chip(k, tok, width), by_slot(row, ff), by_slot(row, ff), by_slot(tok, width),
                       whole((tok, LANES)), whole((tok, fp)), whole((tok, fp)),
                       whole((seq, width)), whole((seq, width))],
            out_shape=[low(local, chips, row, width), low(local, chips, row, ff), low(chips, tok, fp),
                       low(chips, tok, width), low(local, row, ff), low(local, row, ff),
                       low(local, tok, width), shape((tok, LANES), WIDE), low(tok, fp), low(tok, fp),
                       low(seq, width), low(seq, width)],
            scratch_shapes=[pltpu.VMEM((tok, width), WIDE)],
            input_output_aliases={len(fixed) + i: i for i in range(len(store))},
            cost_estimate=cost(flops * 1.2, 6 * local * width * ff),
        )(*fixed, *store)
        store = tuple(out[:4])
        kept.append(out[4:10])
        parts.append(out[10:])
    rows, hidden, s_hidden, second_all = store

    blocks = ring_gather(incoming, blocks)
    back_parts = [None] * chips
    store = ()
    for k in [*range(1, chips), 0]:
        act_a, act_b, picked, probs, s_a, s_b = kept[k]
        store_in = [anywhere] * len(store)
        fixed = (my_slots, *blocks[k], place_row, place_col, probs, picked, act_a, act_b, *weights, s_a, s_b)
        out = pl.pallas_call(
            functools.partial(experts_back_kernel, slot_count),
            grid=(local,),
            in_specs=[smem, whole((seq, width)), whole((seq, width)), *place_specs(k),
                      whole((tok, LANES)), by_slot(tok, width), by_slot(row, ff), by_slot(row, ff),
                      *weight_specs, whole((tok, fp)), whole((tok, fp)), *store_in],
            out_specs=[per_slot(k, row, width), per_slot(k, row, 2 * ff), per_chip(k, tok, 2 * fp),
                       per_chip(k, tok, width), whole((seq, width + LANES)), whole((seq, width + LANES))],
            out_shape=[low(local, chips, row, width), low(local, chips, row, 2 * ff),
                       low(chips, tok, 2 * fp), low(chips, tok, width),
                       low(seq, width + LANES), low(seq, width + LANES)],
            scratch_shapes=[pltpu.VMEM((tok, width), WIDE), pltpu.VMEM((tok, LANES), WIDE)],
            input_output_aliases={len(fixed) + i: i for i in range(len(store))},
            cost_estimate=cost(flops * 1.2, 6 * local * width * ff),
        )(*fixed, *store)
        store = tuple(out[:4])
        back_parts[k] = out[4:]
    grows, g_gu, g_s, up_all = store
    back_sum = ring_sum(back_parts)

    rows, hidden, grows, g_gu = (
        x.reshape(local, chips * row, x.shape[-1]) for x in (rows, hidden, grows, g_gu)
    )
    s_hidden, second_all, g_s, up_all = (
        x.reshape(chips * tok, x.shape[-1]) for x in (s_hidden, second_all, g_s, up_all)
    )

    bits = dp_bits()
    orders = [bits if n % 2 == 0 else bits[::-1] for n in range(local)]
    wide_gu = [dot_rows(rows[n], g_gu[n]).astype(LOW) for n in range(local)]
    wide_gu = [dp_scatter(wide_gu[n], orders[n]) for n in range(local)]

    g_cols = dot_rows(second_all, g_s).astype(LOW)
    grad_sdown = dot_rows(s_hidden, up_all).astype(LOW)[:ff_part]
    g_cols = lax.all_to_all(g_cols.reshape(group, rows_w, 2 * fp), "expert", split_axis=0, concat_axis=0, tiled=True)
    g_cols = g_cols.transpose(1, 0, 2)
    grad_sgate = trim(g_cols[:, :, :fp]).reshape(rows_w, ff)
    grad_sup = trim(g_cols[:, :, fp:]).reshape(rows_w, ff)
    shared_sum = dp_sum(jnp.concatenate([grad_sgate, grad_sup], axis=1))
    sdown_sum = dp_sum(grad_sdown)

    g_middle, g_low, grads_out = pl.pallas_call(
        functools.partial(middle_kernel, routed, slot_count),
        out_shape=[shape((seq, width), WIDE), shape((seq, width), LOW),
                   shape((width, width + LANES), LOW)],
        cost_estimate=cost(2 * seq * width * width, 4 * width * width),
        name="middle_back",
    )(back_sum, second, router, middle, gain_f, incoming, attended)

    grad_tokens, grads_qkv = pl.pallas_call(
        functools.partial(attend_back_kernel, pair),
        grid=(steps,),
        in_specs=[smem, whole((seq, width)), whole((seq, width)), whole((seq, width)),
                  whole((1, width)), whole((seq, HEAD_DIM)), whole((seq, HEAD_DIM)),
                  columns(3 * part), *qkv_specs, pl.BlockSpec((part, width), lambda h: (h, 1))],
        out_specs=[whole((seq, width)), pl.BlockSpec(memory_space=pl.ANY)],
        out_shape=[shape((seq, width), WIDE), shape((width, 3 * width + LANES), LOW)],
        scratch_shapes=[pltpu.VMEM((seq, width), LOW), pltpu.VMEM((seq, width), WIDE),
                        pltpu.VMEM((2, 3, width, part), LOW), pltpu.VMEM((width, LANES), LOW),
                        pltpu.SemaphoreType.DMA((3, 3))],
        cost_estimate=cost(2 * seq * width * 3 * width * 3, 16 * width * width),
        name="attend_back",
    )(lengths, g_low, g_middle, x_low, gain_a, cosine, sine, saved, qk, qk, vo, vo)
    out_sum = lax.psum_scatter(grads_out, "expert", scatter_dimension=0, tiled=True)
    qkv_sum = lax.psum_scatter(grads_qkv, "expert", scatter_dimension=0, tiled=True)
    out_sum = dp_sum(out_sum)
    qkv_sum = dp_sum(qkv_sum)

    hidden, grows, _ = lax.optimization_barrier((hidden, grows, grad_tokens))
    wide_down = [dp_scatter(dot_rows(hidden[n], grows[n]).astype(LOW), orders[n]) for n in range(local)]
    wide_gu, wide_down = jnp.stack(wide_gu), jnp.stack(wide_down)

    parts, _ = after_that(parts, back_sum)
    output = (middle + ring_sum(parts)).astype(LOW)

    def wide(x):
        return x.astype(WIDE)

    return (
        output[None],
        grad_tokens[None],
        wide(qkv_sum[:, 3 * width]),
        wide(qkv_sum[:, :width]),
        wide(qkv_sum[:, width : 2 * width]),
        wide(qkv_sum[:, 2 * width : 3 * width]),
        wide(out_sum[:, :width]),
        wide(out_sum[:, width + routed]),
        wide(shared_sum[:, :ff]),
        wide(shared_sum[:, ff:]),
        wide(sdown_sum),
        wide(out_sum[:, width : width + routed]),
        wide_gu[:, :, :ff],
        wide_gu[:, :, ff:],
        wide_down,
    )


def solution(mesh):
    split = ("dp", "expert")
    e1, e2, e3 = P("expert"), P("expert", None), P("expert", None, None)
    s3 = P(split, None, None)
    scattered = P("expert", "dp", None)

    def step(*args):
        return per_device(*args)

    step = jax.shard_map(
        step,
        mesh=mesh,
        in_specs=(s3, P(split), s3, e1, e2, e2, e2, e2, e1, e2, e2, e2, e2, e3, e3, e3, s3),
        out_specs=(s3, s3, e1, e2, e2, e2, e2, e1, e2, e2, e2, e2) + (scattered,) * 3,
        check_vma=False,
    )
    return step
```

```python
import functools
import math

import jax
import jax.numpy as jnp
from jax import lax
from jax.experimental import pallas as pl
from jax.experimental.pallas import tpu as pltpu
from jax.sharding import PartitionSpec as P


HEAD_DIM = 128
LANES = 128
EPS = 1e-06
LOW = jnp.bfloat16
WIDE = jnp.float32
INT = jnp.int32


def dot(a, b, dims=((1,), (0,))):
    return lax.dot_general(a, b, (dims, ((), ())), preferred_element_type=WIDE)


def dot_t(a, b):
    return dot(a, b, ((1,), (1,)))


def dot_rows(a, b):
    return dot(a, b, ((0,), (0,)))


def inverse_rms(v):
    return lax.rsqrt(jnp.mean(v * v, axis=-1, keepdims=True) + EPS)


def iota(shape, axis):
    return lax.broadcasted_iota(INT, shape, axis)


def lane_pick(x, lane):
    return jnp.sum(jnp.where(iota(x.shape, 1) == lane, x, jnp.zeros_like(x)), axis=1, keepdims=True)


def masked_softmax(logits, count):
    logits = jnp.where(iota(logits.shape, 1) < count, logits, -1e30)
    e = jnp.exp(logits - jnp.max(logits, axis=-1, keepdims=True))
    return e / jnp.sum(e, axis=-1, keepdims=True)


def whole(shape):
    n = len(shape)
    return pl.BlockSpec(shape, lambda *_: (0,) * n, pipeline_mode=pl.Buffered(1))


def cost(flops, size):
    return pl.CostEstimate(flops=int(flops), bytes_accessed=int(size), transcendentals=0)


def turn(v, cosine, sine):
    return v * cosine + pltpu.roll(v, HEAD_DIM // 2, 1) * sine


def head_probs(q, k, allowed):
    s = dot_t(q, k) * (1.0 / math.sqrt(HEAD_DIM))
    s = jnp.where(allowed, s, -1e30)
    e = jnp.exp(s - jnp.max(s, axis=-1, keepdims=True))
    return e * (1.0 / jnp.sum(e, axis=-1, keepdims=True))


def allowed_keys(seq, length):
    key = iota((seq, seq), 1)
    return (key <= iota((seq, seq), 0)) & (key < length)


def attend_kernel(
    pair, turn_over, length_ref, x_ref, gain_ref, cos_ref, sin_ref, wq_ref, wk0_ref, wk1_ref, wv_ref,
    qkv_ref, out_ref, normed,
):
    seq = x_ref.shape[0]
    part = pair * HEAD_DIM

    @pl.when(pl.program_id(0) == 0)
    def _():
        x = x_ref[...].astype(WIDE)
        normed[...] = (x * inverse_rms(x) * gain_ref[...]).astype(LOW)

    wk = jnp.where(pl.program_id(0) < turn_over, wk0_ref[...], wk1_ref[...])
    pre_q, pre_k, pre_v = (dot(normed[...], w) for w in (wq_ref[...], wk, wv_ref[...]))
    allowed = allowed_keys(seq, length_ref[0])
    cosine, sine = cos_ref[...], sin_ref[...]
    for i in range(pair):
        at = i * HEAD_DIM
        q = turn(pre_q[:, at : at + HEAD_DIM], cosine, sine).astype(LOW)
        k = turn(pre_k[:, at : at + HEAD_DIM], cosine, sine).astype(LOW)
        v = pre_v[:, at : at + HEAD_DIM].astype(LOW)
        qkv_ref[:, at : at + HEAD_DIM] = q
        qkv_ref[:, part + at : part + at + HEAD_DIM] = k
        qkv_ref[:, 2 * part + at : 2 * part + at + HEAD_DIM] = v
        p = head_probs(q, k, allowed).astype(LOW)
        out_ref[:, at : at + HEAD_DIM] = dot(p, v).astype(LOW)


def assemble_kernel(rows_ref, columns_ref, *refs):
    *pieces, out_ref, sems = refs
    copies = []
    for n, piece in enumerate(pieces):
        r, c = piece.shape
        place = out_ref.at[
            pl.ds(pl.multiple_of(rows_ref[n] * r, r), r), pl.ds(pl.multiple_of(columns_ref[n] * c, c), c)
        ]
        copies.append(pltpu.make_async_copy(piece, place, sems.at[n]))
    for copy in copies:
        copy.start()
    for copy in copies:
        copy.wait()


def project_kernel(att_ref, w_ref, x_ref, gain_ref, middle_ref, second_ref):
    middle = x_ref[...].astype(WIDE) + dot(att_ref[...], w_ref[...])
    middle_ref[...] = middle
    second_ref[...] = (middle * inverse_rms(middle) * gain_ref[...]).astype(LOW)


def middle_kernel(
    routed, slots, back_ref, second_ref, router_ref, middle_ref, gain_ref, up_ref, att_ref,
    wide_ref, low_ref, grads_ref,
):
    width = middle_ref.shape[1]
    second, router = second_ref[...], router_ref[...]
    probs = masked_softmax(dot(second, router), routed)
    both = back_ref[:, width:]
    lane = iota(both.shape, 1)
    g_gates = jnp.where(lane < routed, both + pltpu.roll(both, LANES - slots, 1), 0.0)
    g_logits = probs * (g_gates - jnp.sum(g_gates * probs, axis=-1, keepdims=True))
    g_logits = g_logits.astype(LOW)
    g_second = back_ref[:, :width] + dot_t(g_logits, router)
    middle = middle_ref[...]
    r = inverse_rms(middle)
    scaled = g_second * gain_ref[...]
    g_norm = r * (scaled - middle * (r * r) * jnp.mean(scaled * middle, axis=-1, keepdims=True))
    g_middle = up_ref[...].astype(WIDE) + g_norm
    wide_ref[...] = g_middle
    low = g_middle.astype(LOW)
    low_ref[...] = low
    grads_ref[:, :width] = dot_rows(att_ref[...], low).astype(LOW)
    g_gain = jnp.sum(g_second * middle * r, axis=0, keepdims=True)
    first = jnp.where(iota((8, width), 0) == 0, jnp.broadcast_to(g_gain, (8, width)), 0.0)
    mark = ((iota((8, LANES), 0) == 0) & (iota((8, LANES), 1) == routed)).astype(LOW)
    grads_ref[:, width:] = (dot_rows(second, g_logits) + dot_rows(first.astype(LOW), mark)).astype(LOW)


def attend_back_kernel(
    pair, turn_over, length_ref, low_ref, wide_ref, x_ref, gain_ref, cos_ref, sin_ref, qkv_ref, wq_ref, wk0_ref, wk1_ref,
    wv_ref, wo_ref, tokens_ref, grads_ref, last_ref, normed, total, ready, gain_ready, sems,
):
    seq, width = x_ref.shape
    part = pair * HEAD_DIM
    step = pl.program_id(0)
    steps = pl.num_programs(0)
    slot = lax.rem(step, 2)

    def leave(n, at):
        copies = []
        for i in range(3):
            columns = pl.ds(pl.multiple_of(i % 2 * width + n * part, LANES), part)
            place = (last_ref if i == 2 else grads_ref).at[:, columns]
            copies.append(pltpu.make_async_copy(ready.at[at, i], place, sems.at[at, i]))
        return copies

    @pl.when(step == 0)
    def _():
        x = x_ref[...].astype(WIDE)
        normed[...] = (x * inverse_rms(x) * gain_ref[...]).astype(LOW)
        total[...] = jnp.zeros_like(total)

    allowed = allowed_keys(seq, length_ref[0])
    cosine, sine = cos_ref[...], sin_ref[...]
    g_att = dot_t(low_ref[...], wo_ref[...]).astype(LOW)
    root = 1.0 / math.sqrt(HEAD_DIM)
    gq, gk, gv = [], [], []
    for i in range(pair):
        at = i * HEAD_DIM
        q = qkv_ref[:, at : at + HEAD_DIM]
        k = qkv_ref[:, part + at : part + at + HEAD_DIM]
        v = qkv_ref[:, 2 * part + at : 2 * part + at + HEAD_DIM]
        ga = g_att[:, at : at + HEAD_DIM]
        p = head_probs(q, k, allowed)
        gp = dot_t(ga, v)
        gv.append(dot_rows(p.astype(LOW), ga))
        ds = (p * (gp - jnp.sum(gp * p, axis=-1, keepdims=True))).astype(LOW)
        gq.append(turn(dot(ds, k) * root, cosine, -sine))
        gk.append(turn(dot_rows(ds, q) * root, cosine, -sine))
    g = jnp.concatenate(gq + gk + gv, axis=1).astype(LOW)

    @pl.when(step >= 2)
    def _():
        for copy in leave(step - 2, slot):
            copy.wait()

    wk = jnp.where(step < turn_over, wk0_ref[...], wk1_ref[...])
    for i, w in enumerate((wq_ref[...], wk, wv_ref[...])):
        piece = g[:, i * part : (i + 1) * part]
        total[...] += dot_t(piece, w)
        ready[slot, i] = dot_rows(normed[...], piece).astype(LOW)
    for copy in leave(step, slot):
        copy.start()

    @pl.when(step == steps - 1)
    def _():
        x = x_ref[...].astype(WIDE)
        r = inverse_rms(x)
        grad = total[...]
        scaled = grad * gain_ref[...]
        back = r * (scaled - x * (r * r) * jnp.mean(scaled * x, axis=-1, keepdims=True))
        tokens_ref[...] = wide_ref[...] + back
        g_gain = jnp.sum(grad * x * r, axis=0, keepdims=True)
        first = jnp.where(iota((8, width), 0) == 0, jnp.broadcast_to(g_gain, (8, width)), 0.0)
        mark = ((iota((8, LANES), 0) == 0) & (iota((8, LANES), 1) == 0)).astype(LOW)
        gain_ready[...] = dot_rows(first.astype(LOW), mark).astype(LOW)
        last = pltpu.make_async_copy(gain_ready, last_ref.at[:, width:], sems.at[2, 0])
        last.start()
        for copy in leave(step - 1, 1 - slot) + leave(step, slot) + [last]:
            copy.wait()


def silu_parts(gate):
    sig = 1.0 / (1.0 + jnp.exp(-gate))
    return gate * sig, sig * (1.0 + gate * (1.0 - sig))


def slots_of(hits, blocks):
    return jnp.concatenate([dot(h, x) for h, x in zip(hits, blocks)], axis=0).astype(LOW)


def row_hits(prow_ref, cap):
    count, _, seq = prow_ref.shape[1:]
    return [
        (iota((cap, seq), 0) == prow_ref[0, i]).astype(WIDE).astype(LOW) for i in range(count)
    ]


def column_hit(pcol_ref, at, e, cap):
    place = lane_pick(pcol_ref[at, :], e)
    return (iota((at.stop - at.start, cap), 1) == place).astype(WIDE).astype(LOW)


def experts_kernel(
    routed, slots_ref, s0_ref, s1_ref, prow_ref, pcol_ref, router_ref, wgu_ref, wd_ref, sc_ref, sd_ref,
    *refs,
):
    (rows_ref, hid_ref, sh_ref, sec_ref, a_ref, b_ref, picked_ref, probs_ref, sa_ref, sb_ref,
     part0_ref, part1_ref, total) = refs[-13:]
    seq, _ = s0_ref.shape
    cap = rows_ref.shape[2] // 2
    ff = wd_ref.shape[1]
    fp = sd_ref.shape[0]
    e = pl.program_id(0)

    @pl.when(e == 0)
    def _():
        sec_ref[0, :seq] = s0_ref[...]
        sec_ref[0, seq:] = s1_ref[...]
        probs_ref[...] = masked_softmax(dot(sec_ref[0], router_ref[...]), routed)
        mid = dot(sec_ref[0], sc_ref[...])
        silu, slope = silu_parts(mid[:, :fp])
        up = mid[:, fp:]
        hidden = (silu * up).astype(LOW)
        sa_ref[...] = silu.astype(LOW)
        sb_ref[...] = (up * slope).astype(LOW)
        sh_ref[0] = hidden
        total[...] = dot(hidden, sd_ref[...])

    slot = slots_ref[e]
    x = slots_of(row_hits(prow_ref, cap), (s0_ref[...], s1_ref[...]))
    rows_ref[0, 0] = x
    mid = dot(x, wgu_ref[0])
    silu, slope = silu_parts(mid[:, :ff])
    up = mid[:, ff:]
    hidden = (silu * up).astype(LOW)
    a_ref[0] = silu.astype(LOW)
    b_ref[0] = (up * slope).astype(LOW)
    hid_ref[0, 0] = hidden
    out = dot(hidden, wd_ref[0])
    for i in range(2):
        at = slice(i * seq, (i + 1) * seq)
        picked = dot(column_hit(pcol_ref, at, e, cap), out[i * cap : (i + 1) * cap].astype(LOW))
        picked_ref[0, at] = picked.astype(LOW)
        total[at, :] += lane_pick(probs_ref[at, :], slot) * picked

    @pl.when(e == pl.num_programs(0) - 1)
    def _():
        part0_ref[...] = total[:seq].astype(LOW)
        part1_ref[...] = total[seq:].astype(LOW)


def experts_back_kernel(
    slot_count, slots_ref, g0_ref, g1_ref, prow_ref, pcol_ref, probs_ref, picked_ref, a_ref, b_ref,
    wgu_ref, wd_ref, sc_ref, sd_ref, sa_ref, sb_ref, *refs,
):
    grows_ref, ggu_ref, gs_ref, up_ref, back0_ref, back1_ref, total, extra = refs[-8:]
    seq, width = g0_ref.shape
    cap = grows_ref.shape[2] // 2
    e = pl.program_id(0)

    @pl.when(e == 0)
    def _():
        up_ref[0, :seq] = g0_ref[...]
        up_ref[0, seq:] = g1_ref[...]
        gh = dot_t(up_ref[0], sd_ref[...])
        gs = jnp.concatenate([gh * sb_ref[...].astype(WIDE), gh * sa_ref[...].astype(WIDE)], axis=1)
        gs = gs.astype(LOW)
        gs_ref[0] = gs
        total[...] = dot_t(gs, sc_ref[...])
        extra[...] = jnp.zeros_like(extra)

    slot = slots_ref[e]
    scaled = []
    for i, g_ref in enumerate((g0_ref, g1_ref)):
        at = slice(i * seq, (i + 1) * seq)
        up = g_ref[...].astype(WIDE)
        scaled.append((lane_pick(probs_ref[at, :], slot) * up).astype(LOW))
        choice = jnp.sum(up * picked_ref[0, at].astype(WIDE), axis=1, keepdims=True)
        high = choice.astype(LOW).astype(WIDE)
        lane = iota((seq, LANES), 1)
        extra[at, :] += jnp.where(
            lane == slot, high, jnp.where(lane == slot + slot_count, choice - high, 0.0)
        )
    x = slots_of(row_hits(prow_ref, cap), scaled)
    grows_ref[0, 0] = x
    gh = dot_t(x, wd_ref[0])
    g = jnp.concatenate([gh * b_ref[0].astype(WIDE), gh * a_ref[0].astype(WIDE)], axis=1)
    g = g.astype(LOW)
    ggu_ref[0, 0] = g
    out = dot_t(g, wgu_ref[0])
    for i in range(2):
        at = slice(i * seq, (i + 1) * seq)
        total[at, :] += dot(column_hit(pcol_ref, at, e, cap), out[i * cap : (i + 1) * cap].astype(LOW))

    @pl.when(e == pl.num_programs(0) - 1)
    def _():
        for i, ref in enumerate((back0_ref, back1_ref)):
            at = slice(i * seq, (i + 1) * seq)
            ref[:, :width] = total[at, :].astype(LOW)
            ref[:, width:] = extra[at, :].astype(LOW)


def around(x):
    count = lax.axis_size("expert")
    return lax.ppermute(x, "expert", [(i, (i + 2) % count) for i in range(count)])


def partner(x):
    count = lax.axis_size("expert")
    return lax.ppermute(x, "expert", [(i, i ^ 1) for i in range(count)])


def add(*xs):
    return sum(x.astype(WIDE) for x in xs)


def ring_gather(x, behind=None):
    blocks = []
    for k in range(lax.axis_size("expert") // 2):
        if k == 2 and behind:
            x, _ = after_that(x, behind[-1][0])
        if k:
            x = around(x)
        blocks.append((x, partner(x)))
    return blocks


def ring_sum(parts, needed=None):
    chips = len(parts)
    total = None
    for k in [*range(1, chips), 0]:
        mine = (parts[k][0], partner(parts[k][1]))
        if total is None:
            total = add(*mine).astype(LOW)
            if needed is not None:
                total, _ = after_that(total, needed)
        else:
            total = around(total)
            total = add(*mine, total)
            total = total.astype(LOW) if k else total
    return total


def exchange(x, bit):
    count = lax.axis_size("dp")
    return lax.ppermute(x, "dp", [(i, i ^ bit) for i in range(count)])


def dp_bits():
    bits, b = [], 1
    while b < lax.axis_size("dp"):
        bits.append(b)
        b *= 2
    return bits


def dp_sum(x):
    bits = dp_bits()
    cut = x.shape[1] // 2 // LANES * LANES
    parts = []
    for piece, order in ((x[:, :cut], bits), (x[:, cut:], bits[::-1])):
        for bit in order:
            got = exchange(piece, bit)
            piece = (piece.astype(WIDE) + got.astype(WIDE)).astype(LOW)
        parts.append(piece)
    return jnp.concatenate(parts, axis=1)


def scatter_leg(x, order, leg):
    bit = order[leg]
    left = sorted(order[leg:], reverse=True)
    me = lax.axis_index("dp")
    if x.ndim == 2:
        x = x.reshape(*(2 for _ in left), x.shape[0] // lax.axis_size("dp"), x.shape[1])
    at = left.index(bit)
    mine = (me // bit) % 2
    kept = lax.dynamic_index_in_dim(x, mine, at, keepdims=False)
    sent = lax.dynamic_index_in_dim(x, 1 - mine, at, keepdims=False)
    return kept, exchange(sent, bit)


def chained(xs, needed):
    return lax.optimization_barrier((xs, needed))[0]


def after_that(x, needed):
    return lax.optimization_barrier((x, needed))


def per_device(
    tokens,
    lengths,
    routes,
    attn_gain,
    query_weight,
    key_weight,
    value_weight,
    out_weight,
    ffn_gain,
    shared_gate,
    shared_up,
    shared_down,
    router_weight,
    expert_gate,
    expert_up,
    expert_down,
    cotangent,
):
    group = lax.axis_size("expert")
    place_of_me = lax.axis_index("expert")
    local = expert_gate.shape[0]
    slot_count = local * group
    seq, width = tokens.shape[1:]
    top = routes.shape[2]
    heads = width // HEAD_DIM
    ff = expert_gate.shape[2]
    ff_part = ff // group
    fp = -(-ff_part // LANES) * LANES
    rows_w = width // group
    capacity = max(2, 3 * seq * top // (2 * slot_count))
    cap = -(-capacity // 8) * 8
    routed = router_weight.shape[1]
    pair = 2
    steps = heads // pair
    part = pair * HEAD_DIM
    shape = jax.ShapeDtypeStruct

    count = lax.axis_size("dp")
    dp = lax.axis_index("dp")
    near = part
    far_local = jnp.concatenate([out_weight, value_weight, key_weight[:, near:]], axis=1)
    strip = far_local.shape[1] // count
    per_row = -(-seq * top // rows_w)
    routes_low = jnp.pad(routes[0].reshape(-1).astype(LOW), (0, per_row * rows_w - seq * top))
    small = jnp.concatenate(
        [router_weight, attn_gain[:, None], ffn_gain[:, None], routes_low.reshape(rows_w, per_row)], axis=1
    )
    small_lanes = -(-small.shape[1] // LANES) * LANES
    small = jnp.pad(small, ((0, 0), (0, small_lanes - small.shape[1])))
    far_part = jnp.concatenate([lax.dynamic_slice_in_dim(far_local, dp * strip, strip, 1), small], axis=1)
    far_part = lax.all_gather(far_part, "expert", axis=0, tiled=True)
    w_gu = jnp.concatenate([expert_gate, expert_up], axis=2)
    far_part = chained(far_part, w_gu)
    far_part, small = far_part[:, :strip], far_part[:, strip:]
    router = jnp.where(jnp.arange(small_lanes, dtype=INT)[None, :] < routed, small, jnp.zeros_like(small))
    router = router[:, :LANES]
    gain_a = small[:, routed].reshape(1, width).astype(WIDE)
    gain_f = small[:, routed + 1].reshape(1, width).astype(WIDE)
    routes_all = small[:, routed + 2 : routed + 2 + per_row].reshape(group, rows_w * per_row)
    routes_all = routes_all[:, : seq * top].reshape(group, seq, top).astype(INT)
    qk = jnp.concatenate([query_weight, key_weight[:, :near]], axis=1)
    qk = lax.all_gather(qk, "expert", axis=0, tiled=True)
    half = width // 2
    core = place_of_me % 2
    first = lax.dynamic_slice_in_dim(far_part, core * half, half, 0)
    if count == 4:
        one, two = exchange(first, 1), exchange(first, 2)
        cut = half // 2
        pieces = [(first, 0, 0), (one, 0, 1), (two, 0, 2),
                  (exchange(one[:cut], 2), 0, 3), (exchange(two[cut:], 1), cut, 3)]
    else:
        pieces = [(first, 0, 0)]
        for bit in dp_bits():
            pieces += [(exchange(p, bit), r, n ^ bit) for p, r, n in pieces]
    placed = []
    for p, r, n in pieces:
        for other, x in enumerate((p, partner(p))):
            rows = x.shape[0]
            placed.append((x, (core ^ other) * (half // rows) + r // rows, dp ^ n))
    smem = pl.BlockSpec(memory_space=pltpu.SMEM)
    far = pl.pallas_call(
        assemble_kernel,
        in_specs=[smem, smem] + [pl.BlockSpec(memory_space=pltpu.VMEM)] * len(placed),
        out_specs=pl.BlockSpec(memory_space=pl.ANY),
        out_shape=pltpu.HBM((width, strip * count), LOW),
        scratch_shapes=[pltpu.SemaphoreType.DMA((len(placed),))],
        cost_estimate=cost(0, 8 * width * width),
        compiler_params=pltpu.CompilerParams(vmem_limit_bytes=24 << 20),
        name="assemble",
    )(jnp.stack([p[1] for p in placed]), jnp.stack([p[2] for p in placed]), *(p[0] for p in placed))

    chips = group // 2
    back = jnp.arange(chips, dtype=INT)[:, None]
    met = 2 * ((place_of_me // 2 - back) % chips) + (core ^ jnp.arange(2, dtype=INT)[None, :])
    routes_all = routes_all[met.reshape(-1)]

    def to_columns(w):
        w = w.reshape(w.shape[0], group, ff_part).transpose(1, 0, 2)
        return jnp.pad(w, ((0, 0), (0, 0), (0, fp - ff_part)))

    def trim(x):
        return x[..., :ff_part]

    cols_local = jnp.concatenate([to_columns(shared_gate), to_columns(shared_up)], axis=2)
    cols_local = chained(cols_local, far_part)
    cols = lax.all_to_all(cols_local, "expert", split_axis=0, concat_axis=0, tiled=True)
    shared_cols = cols.reshape(width, 2 * fp)
    shared_rows = jnp.pad(shared_down, ((0, fp - ff_part), (0, 0)))

    my_slots = place_of_me * local + jnp.arange(local, dtype=INT)
    positions = jnp.arange(seq, dtype=INT)
    member = jnp.any(routes_all[None] == my_slots[:, None, None, None], axis=-1)
    earlier = (positions[:, None] < positions[None, :]).astype(LOW)
    place = jnp.einsum("egb,bt->egt", member.astype(LOW), earlier, preferred_element_type=WIDE)
    place = jnp.where(member, place.astype(INT), -1)
    place_row = place[:, :, None, :]
    place_col = jnp.pad(
        place.reshape(local, group * seq).T, ((0, 0), (0, LANES - local)), constant_values=-1
    )

    halfway = HEAD_DIM // 2
    inverse = 10000.0 ** (-2.0 * jnp.arange(halfway, dtype=WIDE) / HEAD_DIM)
    angles = jnp.arange(seq, dtype=WIDE)[:, None] * inverse[None, :]
    cosine = jnp.tile(jnp.cos(angles), (1, 2))
    sine = jnp.concatenate([-jnp.sin(angles), jnp.sin(angles)], axis=1)

    x_low = tokens[0]
    incoming = cotangent[0]
    early = (shared_rows, w_gu, place_row, place_col, router)
    qk, early = after_that(qk, early)
    incoming, qk = after_that(incoming, qk)
    shared_rows, w_gu, place_row, place_col, router = early

    def columns(n):
        return pl.BlockSpec((seq, n), lambda h: (0, h))

    def stored(*xs):
        return [pltpu.with_memory_space_constraint(x, pltpu.HBM) for x in xs]

    qk, far = stored(qk, far)

    def weight_columns(place):
        return pl.BlockSpec((width, part), lambda h: (0, place(h)))

    turn_over = near // part
    qkv_specs = [weight_columns(lambda h: h),
                 weight_columns(lambda h: steps + jnp.minimum(h, turn_over - 1)),
                 weight_columns(lambda h: 2 * steps + jnp.maximum(h - turn_over, 0)),
                 weight_columns(lambda h: steps + h)]

    saved, attended = pl.pallas_call(
        functools.partial(attend_kernel, pair, turn_over),
        grid=(steps,),
        in_specs=[smem, whole((seq, width)), whole((1, width)), whole((seq, HEAD_DIM)),
                  whole((seq, HEAD_DIM)), *qkv_specs],
        out_specs=[columns(3 * part), columns(part)],
        out_shape=[shape((seq, 3 * width), LOW), shape((seq, width), LOW)],
        scratch_shapes=[pltpu.VMEM((seq, width), LOW)],
        cost_estimate=cost(2 * seq * width * 3 * width * 1.3, 6 * width * width),
        compiler_params=pltpu.CompilerParams(vmem_limit_bytes=24 << 20),
        name="attend",
    )(lengths, x_low, gain_a, cosine, sine, qk, qk, far, far)
    middle, second = pl.pallas_call(
        project_kernel,
        grid=(1,),
        in_specs=[whole((seq, width)), pl.BlockSpec((width, width), lambda _: (0, 0)),
                  whole((seq, width)), whole((1, width))],
        out_specs=[whole((seq, width)), whole((seq, width))],
        out_shape=[shape((seq, width), WIDE), shape((seq, width), LOW)],
        cost_estimate=cost(2 * seq * width * width, 4 * width * width),
        compiler_params=pltpu.CompilerParams(vmem_limit_bytes=24 << 20),
        name="project",
    )(attended, far, x_low, gain_f)

    anywhere = pl.BlockSpec(memory_space=pl.ANY)
    tok, row = 2 * seq, 2 * cap
    flops = 2 * local * row * 3 * width * ff
    weights = (w_gu, expert_down, shared_cols, shared_rows)
    weight_specs = [pl.BlockSpec((1, width, 2 * ff), lambda e: (e, 0, 0)),
                    pl.BlockSpec((1, ff, width), lambda e: (e, 0, 0)),
                    whole((width, 2 * fp)), whole((fp, width))]

    def low(*dims):
        return pltpu.HBM(dims, LOW)

    def per_slot(k, r, n):
        return pl.BlockSpec((1, 1, r, n), lambda e: (e, k, 0, 0))

    def per_chip(k, r, n):
        return pl.BlockSpec((1, r, n), lambda e: (k, 0, 0))

    def by_slot(r, n):
        return pl.BlockSpec((1, r, n), lambda e: (e, 0, 0))

    def place_specs(k):
        return [pl.BlockSpec((1, 2, 1, seq), lambda e: (e, k, 0, 0)),
                pl.BlockSpec((tok, LANES), lambda e: (k, 0))]

    def held(x):
        return pltpu.with_memory_space_constraint(x, pltpu.VMEM)

    weights = (held(w_gu), held(expert_down), shared_cols, shared_rows)
    kept, parts = [], []
    store = ()
    blocks = ring_gather(second)
    for k in range(chips):
        store_in = [anywhere] * len(store)
        fixed = (my_slots, *blocks[k], *stored(place_row, place_col), router, *weights)
        out = pl.pallas_call(
            functools.partial(experts_kernel, routed),
            grid=(local,),
            in_specs=[smem, whole((seq, width)), whole((seq, width)), *place_specs(k),
                      whole((width, LANES)), *weight_specs, *store_in],
            out_specs=[per_slot(k, row, width), per_slot(k, row, ff), per_chip(k, tok, fp),
                       per_chip(k, tok, width), by_slot(row, ff), by_slot(row, ff), by_slot(tok, width),
                       whole((tok, LANES)), whole((tok, fp)), whole((tok, fp)),
                       whole((seq, width)), whole((seq, width))],
            out_shape=[low(local, chips, row, width), low(local, chips, row, ff), low(chips, tok, fp),
                       low(chips, tok, width), low(local, row, ff), low(local, row, ff),
                       low(local, tok, width), pltpu.HBM((tok, LANES), WIDE), low(tok, fp), low(tok, fp),
                       low(seq, width), low(seq, width)],
            scratch_shapes=[pltpu.VMEM((tok, width), WIDE)],
            input_output_aliases={len(fixed) + i: i for i in range(len(store))},
            cost_estimate=cost(flops * 1.2, 6 * local * width * ff),
            compiler_params=pltpu.CompilerParams(vmem_limit_bytes=42 << 20),
        )(*fixed, *stored(*store))
        store = tuple(out[:4])
        kept.append(out[4:10])
        parts.append(out[10:])
    rows, hidden, s_hidden, second_all = store

    blocks = ring_gather(incoming, blocks)
    back_parts = [None] * chips
    store = ()
    for k in [*range(1, chips), 0]:
        act_a, act_b, picked, probs, s_a, s_b = kept[k]
        store_in = [anywhere] * len(store)
        fixed = (my_slots, *blocks[k], *stored(place_row, place_col, probs, picked, act_a, act_b), *weights,
                 *stored(s_a, s_b))
        out = pl.pallas_call(
            functools.partial(experts_back_kernel, slot_count),
            grid=(local,),
            in_specs=[smem, whole((seq, width)), whole((seq, width)), *place_specs(k),
                      whole((tok, LANES)), by_slot(tok, width), by_slot(row, ff), by_slot(row, ff),
                      *weight_specs, whole((tok, fp)), whole((tok, fp)), *store_in],
            out_specs=[per_slot(k, row, width), per_slot(k, row, 2 * ff), per_chip(k, tok, 2 * fp),
                       per_chip(k, tok, width), whole((seq, width + LANES)), whole((seq, width + LANES))],
            out_shape=[low(local, chips, row, width), low(local, chips, row, 2 * ff),
                       low(chips, tok, 2 * fp), low(chips, tok, width),
                       low(seq, width + LANES), low(seq, width + LANES)],
            scratch_shapes=[pltpu.VMEM((tok, width), WIDE), pltpu.VMEM((tok, LANES), WIDE)],
            input_output_aliases={len(fixed) + i: i for i in range(len(store))},
            cost_estimate=cost(flops * 1.2, 6 * local * width * ff),
            compiler_params=pltpu.CompilerParams(vmem_limit_bytes=42 << 20),
        )(*fixed, *stored(*store))
        store = tuple(out[:4])
        back_parts[k] = out[4:]
    grows, g_gu, g_s, up_all = store
    back_sum = ring_sum(back_parts)

    rows, hidden, grows, g_gu = (
        x.reshape(local, chips * row, x.shape[-1]) for x in (rows, hidden, grows, g_gu)
    )
    s_hidden, second_all, g_s, up_all = (
        x.reshape(chips * tok, x.shape[-1]) for x in (s_hidden, second_all, g_s, up_all)
    )

    g_middle, g_low, grads_out = pl.pallas_call(
        functools.partial(middle_kernel, routed, slot_count),
        out_shape=[shape((seq, width), WIDE), shape((seq, width), LOW),
                   shape((width, width + LANES), LOW)],
        cost_estimate=cost(2 * seq * width * width, 4 * width * width),
        name="middle_back",
    )(back_sum, second, router, middle, gain_f, incoming, attended)

    bits = dp_bits()
    orders = [bits if n % 2 == 0 else bits[::-1] for n in range(local)]
    rows, g_gu, _ = lax.optimization_barrier((rows, g_gu, g_low))
    gu = [dot_rows(rows[n], g_gu[n]).astype(LOW) for n in range(local)]
    g_low, gu = after_that(g_low, gu)
    gu = [scatter_leg(gu[n], orders[n], 0) for n in range(local)]

    grad_tokens, grads_qk, grads_v = pl.pallas_call(
        functools.partial(attend_back_kernel, pair, turn_over),
        grid=(steps,),
        in_specs=[smem, whole((seq, width)), whole((seq, width)), whole((seq, width)),
                  whole((1, width)), whole((seq, HEAD_DIM)), whole((seq, HEAD_DIM)),
                  columns(3 * part), *qkv_specs, pl.BlockSpec((part, width), lambda h: (h, 0))],
        out_specs=[whole((seq, width))] + [pl.BlockSpec(memory_space=pl.ANY)] * 2,
        out_shape=[shape((seq, width), WIDE), shape((width, 2 * width), LOW),
                   shape((width, width + LANES), LOW)],
        scratch_shapes=[pltpu.VMEM((seq, width), LOW), pltpu.VMEM((seq, width), WIDE),
                        pltpu.VMEM((2, 3, width, part), LOW), pltpu.VMEM((width, LANES), LOW),
                        pltpu.SemaphoreType.DMA((3, 3))],
        cost_estimate=cost(2 * seq * width * 3 * width * 3, 16 * width * width),
        name="attend_back",
    )(lengths, g_low, g_middle, x_low, gain_a, cosine, sine, saved, qk, qk, far, far, far)
    out_sum = lax.psum_scatter(grads_out, "expert", scatter_dimension=0, tiled=True)
    qk_sum = lax.psum_scatter(grads_qk, "expert", scatter_dimension=0, tiled=True)
    v_sum = lax.psum_scatter(grads_v, "expert", scatter_dimension=0, tiled=True)

    hidden, grows, g_s, s_hidden = chained((hidden, grows, g_s, s_hidden), grad_tokens)
    down = [dot_rows(hidden[n], grows[n]).astype(LOW) for n in range(local)]
    down = [scatter_leg(down[n], orders[n], 0) for n in range(local)]
    g_cols = dot_rows(second_all, g_s).astype(LOW)
    grad_sdown = dot_rows(s_hidden, up_all).astype(LOW)[:ff_part]
    g_all = lax.all_to_all(
        g_cols.reshape(group, rows_w, 2 * fp), "expert", split_axis=0, concat_axis=0, tiled=True
    )

    gu = chained(gu, ([x[0] for x in down], g_cols))
    gu = [scatter_leg(add(*x).astype(LOW), orders[n], 1) for n, x in enumerate(gu)]
    down = chained(down, [x[0] for x in gu])
    down = [scatter_leg(add(*x).astype(LOW), orders[n], 1) for n, x in enumerate(down)]
    g_cols = chained(g_all, [x[0] for x in down]).transpose(1, 0, 2)
    grad_sgate = trim(g_cols[:, :, :fp]).reshape(rows_w, ff)
    grad_sup = trim(g_cols[:, :, fp:]).reshape(rows_w, ff)
    shared_cut = jnp.concatenate([grad_sgate, grad_sup], axis=1)
    gu, down = chained((gu, down), ([x[0] for x in down], shared_cut))
    shared_sum = dp_sum(shared_cut)
    sdown_sum = dp_sum(grad_sdown)
    wide_gu = jnp.stack([add(*x) for x in gu])
    wide_down = jnp.stack([add(*x) for x in down])
    out_sum = dp_sum(out_sum)
    qk_sum = dp_sum(qk_sum)
    v_sum = dp_sum(v_sum)

    output = (middle + ring_sum(parts, back_sum)).astype(LOW)

    def wide(x):
        return x.astype(WIDE)

    return (
        output[None],
        grad_tokens[None],
        wide(v_sum[:, width]),
        wide(qk_sum[:, :width]),
        wide(qk_sum[:, width:]),
        wide(v_sum[:, :width]),
        wide(out_sum[:, :width]),
        wide(out_sum[:, width + routed]),
        wide(shared_sum[:, :ff]),
        wide(shared_sum[:, ff:]),
        wide(sdown_sum),
        wide(out_sum[:, width : width + routed]),
        wide_gu[:, :, :ff],
        wide_gu[:, :, ff:],
        wide_down,
    )


def solution(mesh):
    split = ("dp", "expert")
    e1, e2, e3 = P("expert"), P("expert", None), P("expert", None, None)
    s3 = P(split, None, None)
    scattered = P("expert", "dp", None)

    def step(*args):
        return per_device(*args)

    step = jax.shard_map(
        step,
        mesh=mesh,
        in_specs=(s3, P(split), s3, e1, e2, e2, e2, e2, e1, e2, e2, e2, e2, e3, e3, e3, s3),
        out_specs=(s3, s3, e1, e2, e2, e2, e2, e1, e2, e2, e2, e2) + (scattered,) * 3,
        check_vma=False,
    )
    return step
```

```python
import functools
import math

import jax
import jax.numpy as jnp
from jax import lax
from jax.experimental import pallas as pl
from jax.experimental.pallas import tpu as pltpu
from jax.sharding import PartitionSpec as P


HEAD_DIM = 128
LANES = 128
EPS = 1e-06
LOW = jnp.bfloat16
WIDE = jnp.float32
INT = jnp.int32


def dot(a, b, dims=((1,), (0,))):
    return lax.dot_general(a, b, (dims, ((), ())), preferred_element_type=WIDE)


def dot_t(a, b):
    return dot(a, b, ((1,), (1,)))


def dot_rows(a, b):
    return dot(a, b, ((0,), (0,)))


def inverse_rms(v):
    return lax.rsqrt(jnp.mean(v * v, axis=-1, keepdims=True) + EPS)


def iota(shape, axis):
    return lax.broadcasted_iota(INT, shape, axis)


def lane_pick(x, lane):
    return jnp.sum(jnp.where(iota(x.shape, 1) == lane, x, jnp.zeros_like(x)), axis=1, keepdims=True)


def masked_softmax(logits, count):
    logits = jnp.where(iota(logits.shape, 1) < count, logits, -1e30)
    e = jnp.exp(logits - jnp.max(logits, axis=-1, keepdims=True))
    return e / jnp.sum(e, axis=-1, keepdims=True)


def whole(shape):
    n = len(shape)
    return pl.BlockSpec(shape, lambda *_: (0,) * n, pipeline_mode=pl.Buffered(1))


def cost(flops, size):
    return pl.CostEstimate(flops=int(flops), bytes_accessed=int(size), transcendentals=0)


def turn(v, cosine, sine):
    return v * cosine + pltpu.roll(v, HEAD_DIM // 2, 1) * sine


def head_probs(q, k, allowed):
    s = dot_t(q, k) * (1.0 / math.sqrt(HEAD_DIM))
    s = jnp.where(allowed, s, -1e30)
    e = jnp.exp(s - jnp.max(s, axis=-1, keepdims=True))
    return e * (1.0 / jnp.sum(e, axis=-1, keepdims=True))


def allowed_keys(seq, length):
    key = iota((seq, seq), 1)
    return (key <= iota((seq, seq), 0)) & (key < length)


def attend_kernel(
    pair, turn_over, length_ref, x_ref, gain_ref, cos_ref, sin_ref, wq_ref, wk0_ref, wk1_ref, wv_ref,
    qkv_ref, out_ref, normed,
):
    seq = x_ref.shape[0]
    part = pair * HEAD_DIM

    @pl.when(pl.program_id(0) == 0)
    def _():
        x = x_ref[...].astype(WIDE)
        normed[...] = (x * inverse_rms(x) * gain_ref[...]).astype(LOW)

    wk = jnp.where(pl.program_id(0) < turn_over, wk0_ref[...], wk1_ref[...])
    pre_q, pre_k, pre_v = (dot(normed[...], w) for w in (wq_ref[...], wk, wv_ref[...]))
    allowed = allowed_keys(seq, length_ref[0])
    cosine, sine = cos_ref[...], sin_ref[...]
    for i in range(pair):
        at = i * HEAD_DIM
        q = turn(pre_q[:, at : at + HEAD_DIM], cosine, sine).astype(LOW)
        k = turn(pre_k[:, at : at + HEAD_DIM], cosine, sine).astype(LOW)
        v = pre_v[:, at : at + HEAD_DIM].astype(LOW)
        qkv_ref[:, at : at + HEAD_DIM] = q
        qkv_ref[:, part + at : part + at + HEAD_DIM] = k
        qkv_ref[:, 2 * part + at : 2 * part + at + HEAD_DIM] = v
        p = head_probs(q, k, allowed).astype(LOW)
        out_ref[:, at : at + HEAD_DIM] = dot(p, v).astype(LOW)


def assemble_kernel(rows_ref, columns_ref, *refs):
    *pieces, out_ref, sems = refs
    copies = []
    for n, piece in enumerate(pieces):
        r, c = piece.shape
        place = out_ref.at[
            pl.ds(pl.multiple_of(rows_ref[n] * r, r), r), pl.ds(pl.multiple_of(columns_ref[n] * c, c), c)
        ]
        copies.append(pltpu.make_async_copy(piece, place, sems.at[n]))
    for copy in copies:
        copy.start()
    for copy in copies:
        copy.wait()


def project_kernel(att_ref, w_ref, x_ref, gain_ref, middle_ref, second_ref):
    middle = x_ref[...].astype(WIDE) + dot(att_ref[...], w_ref[...])
    middle_ref[...] = middle
    second_ref[...] = (middle * inverse_rms(middle) * gain_ref[...]).astype(LOW)


def middle_kernel(
    routed, slots, back_ref, second_ref, router_ref, middle_ref, gain_ref, up_ref, att_ref,
    wide_ref, low_ref, grads_ref,
):
    width = middle_ref.shape[1]
    second, router = second_ref[...], router_ref[...]
    probs = masked_softmax(dot(second, router), routed)
    both = back_ref[:, width:]
    lane = iota(both.shape, 1)
    g_gates = jnp.where(lane < routed, both + pltpu.roll(both, LANES - slots, 1), 0.0)
    g_logits = probs * (g_gates - jnp.sum(g_gates * probs, axis=-1, keepdims=True))
    g_logits = g_logits.astype(LOW)
    g_second = back_ref[:, :width] + dot_t(g_logits, router)
    middle = middle_ref[...]
    r = inverse_rms(middle)
    scaled = g_second * gain_ref[...]
    g_norm = r * (scaled - middle * (r * r) * jnp.mean(scaled * middle, axis=-1, keepdims=True))
    g_middle = up_ref[...].astype(WIDE) + g_norm
    wide_ref[...] = g_middle
    low = g_middle.astype(LOW)
    low_ref[...] = low
    grads_ref[:, :width] = dot_rows(att_ref[...], low).astype(LOW)
    g_gain = jnp.sum(g_second * middle * r, axis=0, keepdims=True)
    first = jnp.where(iota((8, width), 0) == 0, jnp.broadcast_to(g_gain, (8, width)), 0.0)
    mark = ((iota((8, LANES), 0) == 0) & (iota((8, LANES), 1) == routed)).astype(LOW)
    grads_ref[:, width:] = (dot_rows(second, g_logits) + dot_rows(first.astype(LOW), mark)).astype(LOW)


def attend_back_kernel(
    pair, turn_over, length_ref, low_ref, wide_ref, x_ref, gain_ref, cos_ref, sin_ref, qkv_ref, wq_ref, wk0_ref, wk1_ref,
    wv_ref, wo_ref, tokens_ref, grads_ref, last_ref, normed, total, ready, gain_ready, sems,
):
    seq, width = x_ref.shape
    part = pair * HEAD_DIM
    step = pl.program_id(0)
    steps = pl.num_programs(0)
    slot = lax.rem(step, 2)

    def leave(n, at):
        copies = []
        for i in range(3):
            columns = pl.ds(pl.multiple_of(i % 2 * width + n * part, LANES), part)
            place = (last_ref if i == 2 else grads_ref).at[:, columns]
            copies.append(pltpu.make_async_copy(ready.at[at, i], place, sems.at[at, i]))
        return copies

    @pl.when(step == 0)
    def _():
        x = x_ref[...].astype(WIDE)
        normed[...] = (x * inverse_rms(x) * gain_ref[...]).astype(LOW)
        total[...] = jnp.zeros_like(total)

    allowed = allowed_keys(seq, length_ref[0])
    cosine, sine = cos_ref[...], sin_ref[...]
    g_att = dot_t(low_ref[...], wo_ref[...]).astype(LOW)
    root = 1.0 / math.sqrt(HEAD_DIM)
    gq, gk, gv = [], [], []
    for i in range(pair):
        at = i * HEAD_DIM
        q = qkv_ref[:, at : at + HEAD_DIM]
        k = qkv_ref[:, part + at : part + at + HEAD_DIM]
        v = qkv_ref[:, 2 * part + at : 2 * part + at + HEAD_DIM]
        ga = g_att[:, at : at + HEAD_DIM]
        p = head_probs(q, k, allowed)
        gp = dot_t(ga, v)
        gv.append(dot_rows(p.astype(LOW), ga))
        ds = (p * (gp - jnp.sum(gp * p, axis=-1, keepdims=True))).astype(LOW)
        gq.append(turn(dot(ds, k) * root, cosine, -sine))
        gk.append(turn(dot_rows(ds, q) * root, cosine, -sine))
    g = jnp.concatenate(gq + gk + gv, axis=1).astype(LOW)

    @pl.when(step >= 2)
    def _():
        for copy in leave(step - 2, slot):
            copy.wait()

    wk = jnp.where(step < turn_over, wk0_ref[...], wk1_ref[...])
    for i, w in enumerate((wq_ref[...], wk, wv_ref[...])):
        piece = g[:, i * part : (i + 1) * part]
        total[...] += dot_t(piece, w)
        ready[slot, i] = dot_rows(normed[...], piece).astype(LOW)
    for copy in leave(step, slot):
        copy.start()

    @pl.when(step == steps - 1)
    def _():
        x = x_ref[...].astype(WIDE)
        r = inverse_rms(x)
        grad = total[...]
        scaled = grad * gain_ref[...]
        back = r * (scaled - x * (r * r) * jnp.mean(scaled * x, axis=-1, keepdims=True))
        tokens_ref[...] = wide_ref[...] + back
        g_gain = jnp.sum(grad * x * r, axis=0, keepdims=True)
        first = jnp.where(iota((8, width), 0) == 0, jnp.broadcast_to(g_gain, (8, width)), 0.0)
        mark = ((iota((8, LANES), 0) == 0) & (iota((8, LANES), 1) == 0)).astype(LOW)
        gain_ready[...] = dot_rows(first.astype(LOW), mark).astype(LOW)
        last = pltpu.make_async_copy(gain_ready, last_ref.at[:, width:], sems.at[2, 0])
        last.start()
        for copy in leave(step - 1, 1 - slot) + leave(step, slot) + [last]:
            copy.wait()


def silu_parts(gate):
    sig = 1.0 / (1.0 + jnp.exp(-gate))
    return gate * sig, sig * (1.0 + gate * (1.0 - sig))


def slots_of(hits, blocks):
    return jnp.concatenate([dot(h, x) for h, x in zip(hits, blocks)], axis=0).astype(LOW)


def row_hits(prow_ref, cap):
    count, _, seq = prow_ref.shape[1:]
    return [
        (iota((cap, seq), 0) == prow_ref[0, i]).astype(WIDE).astype(LOW) for i in range(count)
    ]


def column_hit(pcol_ref, at, e, cap):
    place = lane_pick(pcol_ref[at, :], e)
    return (iota((at.stop - at.start, cap), 1) == place).astype(WIDE).astype(LOW)


def experts_kernel(
    routed, slots_ref, s0_ref, s1_ref, prow_ref, pcol_ref, router_ref, wgu_ref, wd_ref, sc_ref, sd_ref,
    *refs,
):
    (rows_ref, hid_ref, sh_ref, sec_ref, a_ref, b_ref, picked_ref, probs_ref, sa_ref, sb_ref,
     part0_ref, part1_ref, total) = refs[-13:]
    seq, _ = s0_ref.shape
    cap = rows_ref.shape[2] // 2
    ff = wd_ref.shape[1]
    fp = sd_ref.shape[0]
    e = pl.program_id(0)

    @pl.when(e == 0)
    def _():
        sec_ref[0, :seq] = s0_ref[...]
        sec_ref[0, seq:] = s1_ref[...]
        probs_ref[...] = masked_softmax(dot(sec_ref[0], router_ref[...]), routed)
        mid = dot(sec_ref[0], sc_ref[...])
        silu, slope = silu_parts(mid[:, :fp])
        up = mid[:, fp:]
        hidden = (silu * up).astype(LOW)
        sa_ref[...] = silu.astype(LOW)
        sb_ref[...] = (up * slope).astype(LOW)
        sh_ref[0] = hidden
        total[...] = dot(hidden, sd_ref[...])

    slot = slots_ref[e]
    x = slots_of(row_hits(prow_ref, cap), (s0_ref[...], s1_ref[...]))
    rows_ref[0, 0] = x
    mid = dot(x, wgu_ref[0])
    silu, slope = silu_parts(mid[:, :ff])
    up = mid[:, ff:]
    hidden = (silu * up).astype(LOW)
    a_ref[0] = silu.astype(LOW)
    b_ref[0] = (up * slope).astype(LOW)
    hid_ref[0, 0] = hidden
    out = dot(hidden, wd_ref[0])
    for i in range(2):
        at = slice(i * seq, (i + 1) * seq)
        picked = dot(column_hit(pcol_ref, at, e, cap), out[i * cap : (i + 1) * cap].astype(LOW))
        picked_ref[0, at] = picked.astype(LOW)
        total[at, :] += lane_pick(probs_ref[at, :], slot) * picked

    @pl.when(e == pl.num_programs(0) - 1)
    def _():
        part0_ref[...] = total[:seq].astype(LOW)
        part1_ref[...] = total[seq:].astype(LOW)


def experts_back_kernel(
    slot_count, slots_ref, g0_ref, g1_ref, prow_ref, pcol_ref, probs_ref, picked_ref, a_ref, b_ref,
    wgu_ref, wd_ref, sc_ref, sd_ref, sa_ref, sb_ref, *refs,
):
    grows_ref, ggu_ref, gs_ref, up_ref, back0_ref, back1_ref, total, extra = refs[-8:]
    seq, width = g0_ref.shape
    cap = grows_ref.shape[2] // 2
    e = pl.program_id(0)

    @pl.when(e == 0)
    def _():
        up_ref[0, :seq] = g0_ref[...]
        up_ref[0, seq:] = g1_ref[...]
        gh = dot_t(up_ref[0], sd_ref[...])
        gs = jnp.concatenate([gh * sb_ref[...].astype(WIDE), gh * sa_ref[...].astype(WIDE)], axis=1)
        gs = gs.astype(LOW)
        gs_ref[0] = gs
        total[...] = dot_t(gs, sc_ref[...])
        extra[...] = jnp.zeros_like(extra)

    slot = slots_ref[e]
    scaled = []
    for i, g_ref in enumerate((g0_ref, g1_ref)):
        at = slice(i * seq, (i + 1) * seq)
        up = g_ref[...].astype(WIDE)
        scaled.append((lane_pick(probs_ref[at, :], slot) * up).astype(LOW))
        choice = jnp.sum(up * picked_ref[0, at].astype(WIDE), axis=1, keepdims=True)
        high = choice.astype(LOW).astype(WIDE)
        lane = iota((seq, LANES), 1)
        extra[at, :] += jnp.where(
            lane == slot, high, jnp.where(lane == slot + slot_count, choice - high, 0.0)
        )
    x = slots_of(row_hits(prow_ref, cap), scaled)
    grows_ref[0, 0] = x
    gh = dot_t(x, wd_ref[0])
    g = jnp.concatenate([gh * b_ref[0].astype(WIDE), gh * a_ref[0].astype(WIDE)], axis=1)
    g = g.astype(LOW)
    ggu_ref[0, 0] = g
    out = dot_t(g, wgu_ref[0])
    for i in range(2):
        at = slice(i * seq, (i + 1) * seq)
        total[at, :] += dot(column_hit(pcol_ref, at, e, cap), out[i * cap : (i + 1) * cap].astype(LOW))

    @pl.when(e == pl.num_programs(0) - 1)
    def _():
        for i, ref in enumerate((back0_ref, back1_ref)):
            at = slice(i * seq, (i + 1) * seq)
            ref[:, :width] = total[at, :].astype(LOW)
            ref[:, width:] = extra[at, :].astype(LOW)


def around(x):
    count = lax.axis_size("expert")
    return lax.ppermute(x, "expert", [(i, (i + 2) % count) for i in range(count)])


def partner(x):
    count = lax.axis_size("expert")
    return lax.ppermute(x, "expert", [(i, i ^ 1) for i in range(count)])


def add(*xs):
    return sum(x.astype(WIDE) for x in xs)


def ring_gather(x, behind=None):
    blocks = []
    for k in range(lax.axis_size("expert") // 2):
        if k == 2 and behind:
            x, _ = after_that(x, behind[-1][0])
        if k:
            x = around(x)
        blocks.append((x, partner(x)))
    return blocks


def ring_sum(parts, needed=None):
    chips = len(parts)
    total = None
    for k in [*range(1, chips), 0]:
        mine = (parts[k][0], partner(parts[k][1]))
        if total is None:
            total = add(*mine).astype(LOW)
            if needed is not None:
                total, _ = after_that(total, needed)
        else:
            total = around(total)
            total = add(*mine, total)
            total = total.astype(LOW) if k else total
    return total


def exchange(x, bit):
    count = lax.axis_size("dp")
    return lax.ppermute(x, "dp", [(i, i ^ bit) for i in range(count)])


def dp_bits():
    bits, b = [], 1
    while b < lax.axis_size("dp"):
        bits.append(b)
        b *= 2
    return bits


def dp_sum(x, needed=None):
    bits = dp_bits()
    cut = x.shape[1] // 2 // LANES * LANES
    parts = []
    for piece, order in ((x[:, :cut], bits), (x[:, cut:], bits[::-1])):
        for bit in order:
            got = exchange(piece, bit)
            if needed is not None:
                got = chained(got, needed)
            piece = (piece.astype(WIDE) + got.astype(WIDE)).astype(LOW)
        parts.append(piece)
    return jnp.concatenate(parts, axis=1)


def scatter_leg(x, order, leg):
    bit = order[leg]
    left = sorted(order[leg:], reverse=True)
    me = lax.axis_index("dp")
    if x.ndim == 2:
        x = x.reshape(*(2 for _ in left), x.shape[0] // lax.axis_size("dp"), x.shape[1])
    at = left.index(bit)
    mine = (me // bit) % 2
    kept = lax.dynamic_index_in_dim(x, mine, at, keepdims=False)
    sent = lax.dynamic_index_in_dim(x, 1 - mine, at, keepdims=False)
    return kept, exchange(sent, bit)


def dp_scatter(x, axis, order):
    me = lax.axis_index("dp")
    left = list(reversed(dp_bits()))
    x = x.reshape(*x.shape[:axis], *(2 for _ in left), x.shape[axis] // lax.axis_size("dp"), *x.shape[axis + 1 :])
    for bit in order:
        at = axis + left.index(bit)
        mine = (me // bit) % 2
        kept = lax.dynamic_index_in_dim(x, mine, at, keepdims=False)
        sent = lax.dynamic_index_in_dim(x, 1 - mine, at, keepdims=False)
        x = add(kept, exchange(sent, bit)).astype(LOW)
        left.remove(bit)
    return x


def dp_gather(x):
    dp, count = lax.axis_index("dp"), lax.axis_size("dp")
    blocks = [x]
    for bit in dp_bits():
        blocks += [exchange(b, bit) for b in blocks]
    ordered = []
    for n in range(count):
        block = blocks[0]
        for m in range(1, count):
            block = jnp.where((dp ^ n) == m, blocks[m], block)
        ordered.append(block)
    return jnp.concatenate(ordered, axis=0)


def chained(xs, needed):
    return lax.optimization_barrier((xs, needed))[0]


def after_that(x, needed):
    return lax.optimization_barrier((x, needed))


def per_device(
    tokens,
    lengths,
    routes,
    attn_gain,
    query_weight,
    key_weight,
    value_weight,
    out_weight,
    ffn_gain,
    shared_gate,
    shared_up,
    shared_down,
    router_weight,
    expert_gate,
    expert_up,
    expert_down,
    cotangent,
):
    group = lax.axis_size("expert")
    place_of_me = lax.axis_index("expert")
    local = expert_gate.shape[0]
    slot_count = local * group
    seq, width = tokens.shape[1:]
    top = routes.shape[2]
    heads = width // HEAD_DIM
    ff = expert_gate.shape[2]
    ff_part = ff // group
    fp = -(-ff_part // LANES) * LANES
    rows_w = width // group
    capacity = max(2, 3 * seq * top // (2 * slot_count))
    cap = -(-capacity // 8) * 8
    routed = router_weight.shape[1]
    pair = 2
    steps = heads // pair
    part = pair * HEAD_DIM
    shape = jax.ShapeDtypeStruct

    count = lax.axis_size("dp")
    dp = lax.axis_index("dp")
    near = part
    far_local = jnp.concatenate([out_weight, value_weight, key_weight[:, near:]], axis=1)
    strip = far_local.shape[1] // count
    per_row = -(-seq * top // rows_w)
    routes_low = jnp.pad(routes[0].reshape(-1).astype(LOW), (0, per_row * rows_w - seq * top))
    small = jnp.concatenate(
        [router_weight, attn_gain[:, None], ffn_gain[:, None], routes_low.reshape(rows_w, per_row)], axis=1
    )
    small_lanes = -(-small.shape[1] // LANES) * LANES
    small = jnp.pad(small, ((0, 0), (0, small_lanes - small.shape[1])))
    far_part = jnp.concatenate([lax.dynamic_slice_in_dim(far_local, dp * strip, strip, 1), small], axis=1)
    far_part = lax.all_gather(far_part, "expert", axis=0, tiled=True)
    w_gu = jnp.concatenate([expert_gate, expert_up], axis=2)
    far_part = chained(far_part, w_gu)
    far_part, small = far_part[:, :strip], far_part[:, strip:]
    router = jnp.where(jnp.arange(small_lanes, dtype=INT)[None, :] < routed, small, jnp.zeros_like(small))
    router = router[:, :LANES]
    gain_a = small[:, routed].reshape(1, width).astype(WIDE)
    gain_f = small[:, routed + 1].reshape(1, width).astype(WIDE)
    routes_all = small[:, routed + 2 : routed + 2 + per_row].reshape(group, rows_w * per_row)
    routes_all = routes_all[:, : seq * top].reshape(group, seq, top).astype(INT)
    qk = jnp.concatenate([query_weight, key_weight[:, :near]], axis=1)
    qk = lax.all_gather(qk, "expert", axis=0, tiled=True)
    half = width // 2
    core = place_of_me % 2
    first = lax.dynamic_slice_in_dim(far_part, core * half, half, 0)
    if count == 4:
        one, two = exchange(first, 1), exchange(first, 2)
        cut = half // 2
        pieces = [(first, 0, 0), (one, 0, 1), (two, 0, 2),
                  (exchange(one[:cut], 2), 0, 3), (exchange(two[cut:], 1), cut, 3)]
    else:
        pieces = [(first, 0, 0)]
        for bit in dp_bits():
            pieces += [(exchange(p, bit), r, n ^ bit) for p, r, n in pieces]
    placed = []
    for p, r, n in pieces:
        for other, x in enumerate((p, partner(p))):
            rows = x.shape[0]
            placed.append((x, (core ^ other) * (half // rows) + r // rows, dp ^ n))
    smem = pl.BlockSpec(memory_space=pltpu.SMEM)
    far = pl.pallas_call(
        assemble_kernel,
        in_specs=[smem, smem] + [pl.BlockSpec(memory_space=pltpu.VMEM)] * len(placed),
        out_specs=pl.BlockSpec(memory_space=pl.ANY),
        out_shape=pltpu.HBM((width, strip * count), LOW),
        scratch_shapes=[pltpu.SemaphoreType.DMA((len(placed),))],
        cost_estimate=cost(0, 8 * width * width),
        compiler_params=pltpu.CompilerParams(vmem_limit_bytes=24 << 20),
        name="assemble",
    )(jnp.stack([p[1] for p in placed]), jnp.stack([p[2] for p in placed]), *(p[0] for p in placed))

    chips = group // 2
    back = jnp.arange(chips, dtype=INT)[:, None]
    met = 2 * ((place_of_me // 2 - back) % chips) + (core ^ jnp.arange(2, dtype=INT)[None, :])
    routes_all = routes_all[met.reshape(-1)]

    def to_columns(w):
        w = w.reshape(w.shape[0], group, ff_part).transpose(1, 0, 2)
        return jnp.pad(w, ((0, 0), (0, 0), (0, fp - ff_part)))

    def trim(x):
        return x[..., :ff_part]

    cols_local = jnp.concatenate([to_columns(shared_gate), to_columns(shared_up)], axis=2)
    cols_local = chained(cols_local, far_part)
    cols = lax.all_to_all(cols_local, "expert", split_axis=0, concat_axis=0, tiled=True)
    shared_cols = cols.reshape(width, 2 * fp)
    shared_rows = jnp.pad(shared_down, ((0, fp - ff_part), (0, 0)))

    my_slots = place_of_me * local + jnp.arange(local, dtype=INT)
    positions = jnp.arange(seq, dtype=INT)
    member = jnp.any(routes_all[None] == my_slots[:, None, None, None], axis=-1)
    earlier = (positions[:, None] < positions[None, :]).astype(LOW)
    place = jnp.einsum("egb,bt->egt", member.astype(LOW), earlier, preferred_element_type=WIDE)
    place = jnp.where(member, place.astype(INT), -1)
    place_row = place[:, :, None, :]
    place_col = jnp.pad(
        place.reshape(local, group * seq).T, ((0, 0), (0, LANES - local)), constant_values=-1
    )

    halfway = HEAD_DIM // 2
    inverse = 10000.0 ** (-2.0 * jnp.arange(halfway, dtype=WIDE) / HEAD_DIM)
    angles = jnp.arange(seq, dtype=WIDE)[:, None] * inverse[None, :]
    cosine = jnp.tile(jnp.cos(angles), (1, 2))
    sine = jnp.concatenate([-jnp.sin(angles), jnp.sin(angles)], axis=1)

    x_low = tokens[0]
    incoming = cotangent[0]
    early = (shared_rows, w_gu, place_row, place_col, router)
    qk, early = after_that(qk, early)
    incoming, qk = after_that(incoming, qk)
    shared_rows, w_gu, place_row, place_col, router = early

    def columns(n):
        return pl.BlockSpec((seq, n), lambda h: (0, h))

    def held(x):
        return pltpu.with_memory_space_constraint(x, pltpu.VMEM)

    def stored(*xs):
        return [pltpu.with_memory_space_constraint(x, pltpu.HBM) for x in xs]

    qk, far = stored(qk, far)

    def weight_columns(place):
        return pl.BlockSpec((width, part), lambda h: (0, place(h)))

    turn_over = near // part
    qkv_specs = [weight_columns(lambda h: h),
                 weight_columns(lambda h: steps + jnp.minimum(h, turn_over - 1)),
                 weight_columns(lambda h: 2 * steps + jnp.maximum(h - turn_over, 0)),
                 weight_columns(lambda h: steps + h)]

    saved, attended = pl.pallas_call(
        functools.partial(attend_kernel, pair, turn_over),
        grid=(steps,),
        in_specs=[smem, whole((seq, width)), whole((1, width)), whole((seq, HEAD_DIM)),
                  whole((seq, HEAD_DIM)), *qkv_specs],
        out_specs=[columns(3 * part), columns(part)],
        out_shape=[shape((seq, 3 * width), LOW), shape((seq, width), LOW)],
        scratch_shapes=[pltpu.VMEM((seq, width), LOW)],
        cost_estimate=cost(2 * seq * width * 3 * width * 1.3, 6 * width * width),
        compiler_params=pltpu.CompilerParams(vmem_limit_bytes=24 << 20),
        name="attend",
    )(lengths, x_low, gain_a, cosine, sine, qk, qk, far, far)
    middle, second = pl.pallas_call(
        project_kernel,
        grid=(1,),
        in_specs=[whole((seq, width)), pl.BlockSpec((width, width), lambda _: (0, 0)),
                  whole((seq, width)), whole((1, width))],
        out_specs=[whole((seq, width)), whole((seq, width))],
        out_shape=[shape((seq, width), WIDE), shape((seq, width), LOW)],
        cost_estimate=cost(2 * seq * width * width, 4 * width * width),
        compiler_params=pltpu.CompilerParams(vmem_limit_bytes=24 << 20),
        name="project",
    )(attended, far, x_low, gain_f)

    anywhere = pl.BlockSpec(memory_space=pl.ANY)
    tok, row = 2 * seq, 2 * cap
    flops = 2 * local * row * 3 * width * ff
    weights = (w_gu, expert_down, shared_cols, shared_rows)
    weight_specs = [pl.BlockSpec((1, width, 2 * ff), lambda e: (e, 0, 0)),
                    pl.BlockSpec((1, ff, width), lambda e: (e, 0, 0)),
                    whole((width, 2 * fp)), whole((fp, width))]

    def low(*dims):
        return pltpu.HBM(dims, LOW)

    def per_slot(k, r, n):
        return pl.BlockSpec((1, 1, r, n), lambda e: (e, k, 0, 0))

    def per_chip(k, r, n):
        return pl.BlockSpec((1, r, n), lambda e: (k, 0, 0))

    def by_slot(r, n):
        return pl.BlockSpec((1, r, n), lambda e: (e, 0, 0))

    def place_specs(k):
        return [pl.BlockSpec((1, 2, 1, seq), lambda e: (e, k, 0, 0)),
                pl.BlockSpec((tok, LANES), lambda e: (k, 0))]

    weights = (held(w_gu), held(expert_down), shared_cols, shared_rows)
    kept, parts = [], []
    store = ()
    blocks = ring_gather(second)
    for k in range(chips):
        store_in = [anywhere] * len(store)
        own = weights if k else (*stored(w_gu, expert_down), *weights[2:])
        fixed = (my_slots, *blocks[k], *stored(place_row, place_col), router, *own)
        out = pl.pallas_call(
            functools.partial(experts_kernel, routed),
            grid=(local,),
            in_specs=[smem, whole((seq, width)), whole((seq, width)), *place_specs(k),
                      whole((width, LANES)), *weight_specs, *store_in],
            out_specs=[per_slot(k, row, width), per_slot(k, row, ff), per_chip(k, tok, fp),
                       per_chip(k, tok, width), by_slot(row, ff), by_slot(row, ff), by_slot(tok, width),
                       whole((tok, LANES)), whole((tok, fp)), whole((tok, fp)),
                       whole((seq, width)), whole((seq, width))],
            out_shape=[low(local, chips, row, width), low(local, chips, row, ff), low(chips, tok, fp),
                       low(chips, tok, width), low(local, row, ff), low(local, row, ff),
                       low(local, tok, width), pltpu.HBM((tok, LANES), WIDE), low(tok, fp), low(tok, fp),
                       low(seq, width), low(seq, width)],
            scratch_shapes=[pltpu.VMEM((tok, width), WIDE)],
            input_output_aliases={len(fixed) + i: i for i in range(len(store))},
            cost_estimate=cost(flops * 1.2, 6 * local * width * ff),
            compiler_params=pltpu.CompilerParams(vmem_limit_bytes=42 << 20),
        )(*fixed, *stored(*store))
        store = tuple(out[:4])
        kept.append(out[4:10])
        parts.append(out[10:])
    rows, hidden, s_hidden, second_all = store

    blocks = ring_gather(incoming, blocks)
    back_parts = [None] * chips
    store = ()
    for k in [*range(1, chips), 0]:
        act_a, act_b, picked, probs, s_a, s_b = kept[k]
        store_in = [anywhere] * len(store)
        fixed = (my_slots, *blocks[k], *stored(place_row, place_col, probs, picked, act_a, act_b), *weights,
                 *stored(s_a, s_b))
        out = pl.pallas_call(
            functools.partial(experts_back_kernel, slot_count),
            grid=(local,),
            in_specs=[smem, whole((seq, width)), whole((seq, width)), *place_specs(k),
                      whole((tok, LANES)), by_slot(tok, width), by_slot(row, ff), by_slot(row, ff),
                      *weight_specs, whole((tok, fp)), whole((tok, fp)), *store_in],
            out_specs=[per_slot(k, row, width), per_slot(k, row, 2 * ff), per_chip(k, tok, 2 * fp),
                       per_chip(k, tok, width), whole((seq, width + LANES)), whole((seq, width + LANES))],
            out_shape=[low(local, chips, row, width), low(local, chips, row, 2 * ff),
                       low(chips, tok, 2 * fp), low(chips, tok, width),
                       low(seq, width + LANES), low(seq, width + LANES)],
            scratch_shapes=[pltpu.VMEM((tok, width), WIDE), pltpu.VMEM((tok, LANES), WIDE)],
            input_output_aliases={len(fixed) + i: i for i in range(len(store))},
            cost_estimate=cost(flops * 1.2, 6 * local * width * ff),
            compiler_params=pltpu.CompilerParams(vmem_limit_bytes=42 << 20),
        )(*fixed, *stored(*store))
        store = tuple(out[:4])
        back_parts[k] = out[4:]
    grows, g_gu, g_s, up_all = store
    back_sum = ring_sum(back_parts)

    rows, hidden, grows, g_gu = (
        x.reshape(local, chips * row, x.shape[-1]) for x in (rows, hidden, grows, g_gu)
    )
    s_hidden, second_all, g_s, up_all = (
        x.reshape(chips * tok, x.shape[-1]) for x in (s_hidden, second_all, g_s, up_all)
    )

    g_middle, g_low, grads_out = pl.pallas_call(
        functools.partial(middle_kernel, routed, slot_count),
        out_shape=[shape((seq, width), WIDE), shape((seq, width), LOW),
                   shape((width, width + LANES), LOW)],
        cost_estimate=cost(2 * seq * width * width, 4 * width * width),
        name="middle_back",
    )(back_sum, second, router, middle, gain_f, incoming, attended)

    bits = dp_bits()
    orders = [bits if n % 2 == 0 else bits[::-1] for n in range(local)]
    rows, g_gu, _ = lax.optimization_barrier((rows, g_gu, g_low))
    gu = [dot_rows(rows[n], g_gu[n]).astype(LOW) for n in range(local)]
    g_low, gu = after_that(g_low, gu)
    gu = [scatter_leg(gu[n], orders[n], 0) for n in range(local)]

    grad_tokens, grads_qk, grads_v = pl.pallas_call(
        functools.partial(attend_back_kernel, pair, turn_over),
        grid=(steps,),
        in_specs=[smem, whole((seq, width)), whole((seq, width)), whole((seq, width)),
                  whole((1, width)), whole((seq, HEAD_DIM)), whole((seq, HEAD_DIM)),
                  columns(3 * part), *qkv_specs, pl.BlockSpec((part, width), lambda h: (h, 0))],
        out_specs=[whole((seq, width))] + [pl.BlockSpec(memory_space=pl.ANY)] * 2,
        out_shape=[shape((seq, width), WIDE), shape((width, 2 * width), LOW),
                   shape((width, width + LANES), LOW)],
        scratch_shapes=[pltpu.VMEM((seq, width), LOW), pltpu.VMEM((seq, width), WIDE),
                        pltpu.VMEM((2, 3, width, part), LOW), pltpu.VMEM((width, LANES), LOW),
                        pltpu.SemaphoreType.DMA((3, 3))],
        cost_estimate=cost(2 * seq * width * 3 * width * 3, 16 * width * width),
        name="attend_back",
    )(lengths, g_low, g_middle, x_low, gain_a, cosine, sine, saved, qk, qk, far, far, far)
    out_sum = lax.psum_scatter(grads_out, "expert", scatter_dimension=0, tiled=True)
    qk_sum = lax.psum_scatter(grads_qk, "expert", scatter_dimension=0, tiled=True)
    v_sum = lax.psum_scatter(grads_v, "expert", scatter_dimension=0, tiled=True)

    hidden, grows, g_s, s_hidden = chained((hidden, grows, g_s, s_hidden), grad_tokens)
    down = [dot_rows(hidden[n], grows[n]).astype(LOW) for n in range(local)]
    down = [scatter_leg(down[n], orders[n], 0) for n in range(local)]
    g_cols = dot_rows(second_all, g_s).astype(LOW)
    grad_sdown = dot_rows(s_hidden, up_all).astype(LOW)[:ff_part]
    parts_of_rows = [
        dp_scatter(g_cols[:, at : at + fp].reshape(group, rows_w, fp), 1, order)
        for at, order in ((0, bits), (fp, bits[::-1]))
    ]
    g_all = lax.all_to_all(jnp.concatenate(parts_of_rows, axis=2), "expert", split_axis=0, concat_axis=0, tiled=True)

    gu = chained(gu, ([x[0] for x in down], g_cols))
    gu = [scatter_leg(add(*x).astype(LOW), orders[n], 1) for n, x in enumerate(gu)]
    down = chained(down, [x[0] for x in gu])
    down = [scatter_leg(add(*x).astype(LOW), orders[n], 1) for n, x in enumerate(down)]
    g_all = g_all.transpose(1, 0, 2)
    shared_cut = jnp.concatenate(
        [trim(g_all[:, :, at : at + fp]).reshape(rows_w // count, ff) for at in (0, fp)], axis=1
    )
    gu, down = chained((gu, down), ([x[0] for x in down], qk_sum))
    shared_sum = dp_gather(shared_cut)
    sdown_sum = dp_sum(grad_sdown, qk_sum)
    wide_gu = jnp.stack([add(*x) for x in gu])
    wide_down = jnp.stack([add(*x) for x in down])
    out_sum = dp_sum(out_sum)
    qk_sum = dp_sum(qk_sum)
    v_sum = dp_sum(v_sum)

    output = (middle + ring_sum(parts, back_sum)).astype(LOW)

    def wide(x):
        return x.astype(WIDE)

    return (
        output[None],
        grad_tokens[None],
        wide(v_sum[:, width]),
        wide(qk_sum[:, :width]),
        wide(qk_sum[:, width:]),
        wide(v_sum[:, :width]),
        wide(out_sum[:, :width]),
        wide(out_sum[:, width + routed]),
        wide(shared_sum[:, :ff]),
        wide(shared_sum[:, ff:]),
        wide(sdown_sum),
        wide(out_sum[:, width : width + routed]),
        wide_gu[:, :, :ff],
        wide_gu[:, :, ff:],
        wide_down,
    )


def solution(mesh):
    split = ("dp", "expert")
    e1, e2, e3 = P("expert"), P("expert", None), P("expert", None, None)
    s3 = P(split, None, None)
    scattered = P("expert", "dp", None)

    def step(*args):
        return per_device(*args)

    step = jax.shard_map(
        step,
        mesh=mesh,
        in_specs=(s3, P(split), s3, e1, e2, e2, e2, e2, e1, e2, e2, e2, e2, e3, e3, e3, s3),
        out_specs=(s3, s3, e1, e2, e2, e2, e2, e1, e2, e2, e2, e2) + (scattered,) * 3,
        check_vma=False,
    )
    return step
```
